256 devices in a mesh: dp: 16 (over x, y), expert: 16 (over z, core).
Axes of the slice: x: 4, y: 4, z: 8, core: 2. Of those that a mesh axis runs over, the one named last changes fastest.
Arguments:
- cotangent: bfloat16 [32768, 4096], P(('dp', 'expert')), may hold values from -6 to 6
- hidden: bfloat16 [16, 16, 256, 768], P('dp', 'expert'), may hold values from -6 to 6
- down_matrix: bfloat16 [16, 4096, 768], P('expert'), may hold values from -0.21875 to 0.21875
- adapter_in: bfloat16 [2, 128, 768], replicated, may hold values from -0.21875 to 0.21875
- adapter_out: bfloat16 [2, 4096, 128], replicated, may hold values from -0.5 to 0.5
- probs: bfloat16 [32768, 8], P(('dp', 'expert')), may hold values from 0.019897461 to 0.5
- routes: int32 [32768, 8], P(('dp', 'expert')), may hold values from 0 to 127, as said below
- token_loop: int32 [32768], P(('dp', 'expert')), may hold values from 0 to 1
Outputs:
- hidden_gradient: bfloat16 [16, 16, 256, 768], P('dp', 'expert')
- down_matrix_gradient: float32 [16, 4096, 768], P('expert', 'dp')
- combine_weight_gradient: float32 [32768, 8], P(('dp', 'expert'))
- adapter_in_gradient: float32 [2, 128, 768], P(None, 'expert', 'dp')
- adapter_out_gradient: float32 [2, 4096, 128], P(None, 'dp', 'expert')
The draws below stay inside these ranges and needn't reach their ends.
Inputs may be any that keep to these rules, and one draw needn't show every extreme that they name: `routes`: each row names 8 different experts. In the 128 rows of one device every expert below 16 is named by 4 to 16 rows, and within each index of dp one such expert is named by exactly 16 rows of every device.
All inputs are finite; a program needn't handle non-finite values.
Results may differ from the reference program's by a relative error of at most 0.0049.
Values may be sent and summed in bfloat16 or wider, within the bound.
A program may use at most 128 MiB of HBM per device.

```python
import math
from functools import partial
import jax
import jax.numpy as jnp
from jax import lax

MODEL_DIM = 4096
HIDDEN_UNITS = 768
EXPERTS = 128
EXPERTS_PER_TOKEN = 8
ADAPTER_RANK = 128
LOOP_TOTAL = 2
TOK_DEV = 128
SLOT_CAPACITY = 16
TOKEN_TOTAL = 32768
N_DP = 16
N_EXPERT = 16


def draw_routes(key, part):
    groups = N_DP
    owner_devices = N_EXPERT
    blocks = groups * owner_devices
    key_full, key_count, key_shuffle, key_fill, key_column = jax.random.split(key, 5)
    full_expert = jax.random.randint(key_full, (groups,), 0, owner_devices)
    lowest = max(1, SLOT_CAPACITY // 4)
    counts = jax.random.randint(key_count, (groups, owner_devices, owner_devices), lowest, SLOT_CAPACITY + 1)
    experts = jnp.arange(owner_devices, dtype=jnp.int32)
    counts = jnp.where(experts[None, None, :] == full_expert[:, None, None], SLOT_CAPACITY, counts).reshape(blocks, owner_devices)
    position = jnp.arange(TOK_DEV, dtype=jnp.int32)
    offset = (position[:, None] - experts[None, :] * SLOT_CAPACITY) % TOK_DEV
    covered = offset[None, :, :] < counts[:, None, :]
    covered_count = covered.astype(jnp.int32)
    order_rank = jnp.cumsum(covered_count, axis=2) - covered_count
    row_count = jnp.sum(covered_count, axis=2)
    column = jnp.arange(EXPERTS_PER_TOKEN, dtype=jnp.int32)
    chosen = covered[:, :, None, :] & (order_rank[:, :, None, :] == column[None, None, :, None])
    window_id = jnp.sum(jnp.where(chosen, experts[None, None, None, :], 0), axis=3)
    remaining = EXPERTS - owner_devices
    fill_start = jax.random.randint(key_fill, (blocks, TOK_DEV, 1), 0, remaining)
    filler = owner_devices + (fill_start + column[None, None, :]) % remaining
    table = jnp.where(column[None, None, :] < row_count[:, :, None], window_id, filler)
    sort_keys = jax.random.randint(key_column, (blocks, TOK_DEV, EXPERTS_PER_TOKEN), 0, 1 << 20) * EXPERTS_PER_TOKEN + column[None, None, :]
    column_order = jnp.argsort(sort_keys, axis=2)
    table = jnp.take_along_axis(table, column_order, axis=2)
    shuffled = jax.vmap(lambda one_key: jax.random.permutation(one_key, TOK_DEV))(jax.random.split(key_shuffle, blocks))
    routed = jnp.take_along_axis(table, shuffled[:, :, None], axis=1)
    return routed.reshape(blocks * TOK_DEV, EXPERTS_PER_TOKEN).astype(jnp.int32)


def touch_ends(entries, own_key, low, high):
    spot = [jax.random.randint(jax.random.fold_in(own_key, axis), (), 0, length) for axis, length in enumerate(entries.shape)]
    main_axis = entries.shape.index(max(entries.shape))
    neighbour = spot[:main_axis] + [(spot[main_axis] + 1) % entries.shape[main_axis]] + spot[main_axis + 1:]
    return entries.at[tuple(spot)].set(low).at[tuple(neighbour)].set(high)


def shard_levels(own_key, shape, cuts, least, largest):
    gain, own = 1.0, jax.random.fold_in(own_key, 6)
    for axis_at, parts in cuts:
        steps = jnp.exp(jax.random.uniform(jax.random.fold_in(own, axis_at), (parts,), jnp.float32, least / len(cuts), largest / len(cuts)))
        gain = gain * jnp.repeat(steps, shape[axis_at] // parts).reshape([-1 if axis == axis_at else 1 for axis in range(len(shape))])
    return gain


def noise(rng, dims, scale, limit, pieces=(), kind=jnp.bfloat16):
    gain = shard_levels(rng, dims, pieces, -0.22, 0.18) if pieces else 1.0
    values = jax.random.normal(rng, dims, jnp.float32) * scale * gain
    return jnp.minimum(jnp.maximum(values, -limit), limit).astype(kind)


def setup_inputs(seed: int = 0) -> dict:
    keys = jax.random.split(jax.random.key(seed), 9)
    return {
        "cotangent": noise(keys[0], (TOKEN_TOTAL, MODEL_DIM), 1.0, 6.0, ((0, 256),)),
        "hidden": noise(keys[1], (N_DP, N_EXPERT, N_EXPERT * SLOT_CAPACITY, HIDDEN_UNITS), 1.0, 6.0, ((0, 16), (1, 16))),
        "down_matrix": noise(keys[2], (N_EXPERT, MODEL_DIM, HIDDEN_UNITS), HIDDEN_UNITS ** -0.5, 0.21875, ((0, 16),)),
        "adapter_in": noise(keys[3], (LOOP_TOTAL, ADAPTER_RANK, HIDDEN_UNITS), HIDDEN_UNITS ** -0.5, 0.21875),
        "adapter_out": noise(keys[4], (LOOP_TOTAL, MODEL_DIM, ADAPTER_RANK), ADAPTER_RANK ** -0.5, 0.5),
        "probs": jnp.clip(jnp.exp(math.log(0.5) - 3.224016 * jax.random.uniform(keys[5], (TOKEN_TOTAL, EXPERTS_PER_TOKEN), jnp.float32) ** shard_levels(keys[5], (TOKEN_TOTAL, EXPERTS_PER_TOKEN), ((0, 256),), -0.2, 0.2)), 0.019897461, 0.5).astype(jnp.bfloat16),
        "routes": draw_routes(jax.random.fold_in(keys[8], 71), 0),
        "token_loop": touch_ends(jax.random.randint(keys[7], (TOKEN_TOTAL,), 0, LOOP_TOTAL), jax.random.fold_in(keys[7], 1), 0, LOOP_TOTAL - 1).astype(jnp.int32),
    }


def route_slots(routes, owner_devices, slot_capacity):
    experts = jnp.arange(owner_devices, dtype=jnp.int32)
    named_count = jnp.sum((routes[:, :, None] == experts[None, None, :]).astype(jnp.int32), axis=1)
    before = jnp.cumsum(named_count, axis=0) - named_count
    in_window = routes < owner_devices
    target = jnp.where(in_window, routes, 0).astype(jnp.int32)
    column = jnp.take_along_axis(before, target, axis=1)
    slot_index = jnp.where(in_window, target * slot_capacity + column, owner_devices * slot_capacity).astype(jnp.int32)
    return in_window, slot_index


def sender_portion(sender_output_gradient, sender_combine_weights, sender_routing, sender_loop, adapter_out_float, owner_devices, slot_capacity):
    slot_count = owner_devices * slot_capacity
    tokens_here = sender_output_gradient.shape[0]
    loop_number = adapter_out_float.shape[0]
    in_window, slot_index = route_slots(sender_routing, owner_devices, slot_capacity)
    token_index = jnp.broadcast_to(jnp.arange(tokens_here, dtype=jnp.int32)[:, None], slot_index.shape)
    slot_token = jnp.full((slot_count,), tokens_here, jnp.int32).at[slot_index.reshape(-1)].set(token_index.reshape(-1), mode="drop")
    slot_weight = jnp.zeros((slot_count,), jnp.float32).at[slot_index.reshape(-1)].set(sender_combine_weights.astype(jnp.float32).reshape(-1), mode="drop")
    loop_mask = (sender_loop[:, None] == jnp.arange(loop_number, dtype=jnp.int32)[None, :]).astype(jnp.float32)
    every_loop = jnp.einsum("xn,jnr->xjr", sender_output_gradient.astype(jnp.float32), adapter_out_float)
    projected = jnp.sum(every_loop * loop_mask[:, :, None], axis=1).astype(jnp.bfloat16)
    padded_dy = jnp.concatenate([sender_output_gradient, jnp.zeros((1, sender_output_gradient.shape[1]), jnp.bfloat16)], axis=0)
    padded_mask = jnp.concatenate([loop_mask, jnp.zeros((1, loop_number), jnp.float32)], axis=0)
    padded_proj = jnp.concatenate([projected, jnp.zeros((1, projected.shape[1]), jnp.bfloat16)], axis=0)
    return (padded_dy[slot_token], slot_weight, padded_mask[slot_token], padded_proj[slot_token], in_window, slot_index, loop_mask)


def finish(in_window, slot_index, back_mix, back_down, sender_output_gradient, loop_mask):
    position = jnp.minimum(slot_index, back_mix.shape[0] - 1)
    combine_weight_gradient = jnp.where(in_window, back_mix[position], 0.0)
    pulled = back_down[position]
    summed = jnp.sum(jnp.where(in_window[:, :, None], pulled, 0.0), axis=1)
    summed = lax.optimization_barrier(summed.astype(jnp.bfloat16)).astype(jnp.float32)
    masked_sum = summed[:, None, :] * loop_mask[:, :, None]
    grad_out = jnp.einsum("td,tlk->ldk", sender_output_gradient.astype(jnp.float32), masked_sum)
    return combine_weight_gradient, grad_out


def reference(cotangent, hidden, down_matrix, adapter_in, adapter_out, probs, routes, token_loop):
    owner_devices = N_EXPERT
    groups = N_DP
    slot_count = owner_devices * SLOT_CAPACITY
    down_matrix_float = down_matrix.astype(jnp.float32)
    adapter_in_float = adapter_in.astype(jnp.float32)
    adapter_out_float = adapter_out.astype(jnp.float32)
    inputs = (cotangent.reshape(groups, owner_devices, TOK_DEV, MODEL_DIM), probs.reshape(groups, owner_devices, TOK_DEV, EXPERTS_PER_TOKEN), routes.reshape(groups, owner_devices, TOK_DEV, EXPERTS_PER_TOKEN), token_loop.reshape(groups, owner_devices, TOK_DEV), hidden)
    per_sender = jax.vmap(partial(sender_portion, adapter_out_float=adapter_out_float, owner_devices=owner_devices, slot_capacity=SLOT_CAPACITY))

    def to_owner(values):
        shaped = values.reshape((owner_devices, owner_devices, SLOT_CAPACITY) + values.shape[2:])
        return jnp.swapaxes(shaped, 0, 1).reshape((owner_devices, slot_count) + values.shape[2:])

    def one_group(running, group_inputs):
        sum_weight, sum_in, sum_out = running
        group_dy, group_probs, group_routes, group_loop, group_hidden = group_inputs
        slot_dy, slot_weight, slot_mask, slot_proj, in_window, slot_index, loop_mask = per_sender(group_dy, group_probs, group_routes, group_loop)
        owner_output_gradient = to_owner(slot_dy).astype(jnp.float32)
        owner_weight = to_owner(slot_weight)
        owner_mask = to_owner(slot_mask)
        owner_proj = to_owner(slot_proj).astype(jnp.float32)
        hidden_float = group_hidden.astype(jnp.float32)
        masked_projection = owner_proj[:, :, None, :] * owner_mask[:, :, :, None]
        input_gradient = jnp.einsum("wug,wgh->wuh", owner_output_gradient, down_matrix_float) + jnp.einsum("phiq,iqt->pht", masked_projection, adapter_in_float)
        hidden_gradient = (owner_weight[:, :, None] * input_gradient).astype(jnp.bfloat16)
        grad_mix = jnp.sum(hidden_float * input_gradient, axis=2)
        scaled = lax.optimization_barrier((owner_weight[:, :, None] * owner_output_gradient).astype(jnp.bfloat16)).astype(jnp.float32)
        sum_weight = sum_weight + jnp.einsum("erd,erf->edf", scaled, hidden_float)
        weighted_proj = lax.optimization_barrier((owner_weight[:, :, None] * owner_proj).astype(jnp.bfloat16)).astype(jnp.float32)
        masked_weighted = weighted_proj[:, :, None, :] * owner_mask[:, :, :, None]
        sum_in = sum_in + jnp.einsum("erlk,erf->lkf", masked_weighted, hidden_float)
        down_weight_stack = jnp.einsum("jog,hpg->johp", hidden_float, adapter_in_float)
        weighted_down = owner_weight[:, :, None] * jnp.sum(down_weight_stack * owner_mask[:, :, :, None], axis=2)
        back_mix = to_owner(grad_mix)
        back_down = to_owner(weighted_down)
        combine_weight_gradient, grad_out = jax.vmap(finish)(in_window, slot_index, back_mix, back_down, group_dy, loop_mask)
        sum_out = sum_out + jnp.sum(grad_out, axis=0)
        return (sum_weight, sum_in, sum_out), (hidden_gradient, combine_weight_gradient)

    start_state = (jnp.zeros((owner_devices, MODEL_DIM, HIDDEN_UNITS), jnp.float32), jnp.zeros((LOOP_TOTAL, ADAPTER_RANK, HIDDEN_UNITS), jnp.float32), jnp.zeros((LOOP_TOTAL, MODEL_DIM, ADAPTER_RANK), jnp.float32))
    closing_state, stacked = lax.scan(one_group, start_state, inputs)
    down_matrix_gradient, adapter_in_gradient, adapter_out_gradient = closing_state
    hidden_gradient, combine_weight_gradient = stacked
    return (hidden_gradient, down_matrix_gradient, combine_weight_gradient.reshape(TOKEN_TOTAL, EXPERTS_PER_TOKEN), adapter_in_gradient, adapter_out_gradient)
```

```python
import functools

import jax
import jax.numpy as jnp
from jax import lax
from jax.experimental import pallas as pl
from jax.experimental.pallas import tpu as pltpu
from jax.sharding import PartitionSpec as P

MESH = pl.DeviceIdType.MESH
F32 = jnp.float32
BF16 = jnp.bfloat16

NX = 4
NY = 4
NE = 16
CAP = 16
TOK = 128
SLOTS = NE * CAP
MODEL = 4096
HID = 768
RANK = 128
EXT = 2 * RANK
ROWS = MODEL // (NX * NY)
ACOL = HID // (NX * NY)

STEPS = ((1, 0, 256), (2, 0, 256), (3, 0, 256), (0, 0, 128), (0, 128, 128))
NS = len(STEPS)


def rcopy(src, dst, send, recv, dev):
    return pltpu.make_async_remote_copy(
        src_ref=src, dst_ref=dst, send_sem=send, recv_sem=recv, device_id=dev, device_id_type=MESH
    )


def dot(a, b):
    return jnp.dot(a, b, preferred_element_type=F32)


def kernel(cot_h, hid_h, w_h, ain_h, aout_h, probs_ref, routes_ref, loop_ref, *refs):
    hg_ref, dw_ref, cwg_ref, ga_ref, gb_ref = refs[:5]
    (cot, aout, ain, wm, hx, dx, aperm, sbuf, mbuf, acc, sel) = refs[5:16]
    (msend, mrecv, q1s, q1r, q2s, q2r, rzs, rzr, xs_, xr_, gzs, gzr, ps, pr, own) = refs[16:31]
    dys = refs[31 : 31 + NS]
    dyr = refs[31 + NS : 31 + 2 * NS]
    tsd = refs[31 + 2 * NS : 31 + 3 * NS]
    trv = refs[31 + 3 * NS : 31 + 4 * NS]
    (lsem, dy_s, dy_r, m_s, m_r, x_s, x_r, y_s, y_r, z_s, z_r) = refs[31 + 4 * NS :]

    dp = lax.axis_index("dp")
    e = lax.axis_index("expert")
    x = dp // NY
    y = lax.rem(dp, NY)

    def zdev(p):
        return (dp, p)

    def xdev(p):
        return (p * NY + y, e)

    def ydev(p):
        return (x * NY + p, e)

    loads = [
        pltpu.make_async_copy(cot_h, cot, lsem.at[0]),
        pltpu.make_async_copy(hid_h, hx.at[x], lsem.at[1]),
        pltpu.make_async_copy(aout_h, aout, lsem.at[2]),
        pltpu.make_async_copy(ain_h, ain, lsem.at[3]),
        pltpu.make_async_copy(w_h, wm, lsem.at[4]),
    ]
    for one in loads:
        one.start()

    barrier = pltpu.get_barrier_semaphore()

    def greet_z(k, c):
        pl.semaphore_signal(barrier, inc=1, device_id=zdev(lax.rem(e + k, NE)), device_id_type=MESH)
        return c

    lax.fori_loop(1, NE, greet_z, 0)
    for k in range(1, NX):
        pl.semaphore_signal(barrier, inc=1, device_id=xdev(lax.rem(x + k, NX)), device_id_type=MESH)
        pl.semaphore_signal(barrier, inc=1, device_id=ydev(lax.rem(y + k, NY)), device_id_type=MESH)

    routes = routes_ref[...]
    probs = probs_ref[...].astype(F32)
    expert_id = lax.broadcasted_iota(jnp.int32, (NE, TOK), 0)
    named = jnp.zeros((NE, TOK), F32)
    weight = jnp.zeros((NE, TOK), F32)
    for k in range(8):
        hit = (routes[k : k + 1, :] == expert_id).astype(F32)
        named = named + hit
        weight = weight + hit * probs[k : k + 1, :]
    row = lax.broadcasted_iota(jnp.int32, (TOK, TOK), 0)
    col = lax.broadcasted_iota(jnp.int32, (TOK, TOK), 1)
    before = dot(named.astype(BF16), (row < col).astype(F32).astype(BF16))
    before = jnp.where(named > 0.5, before, -1.0)
    place = lax.broadcasted_iota(jnp.int32, (NE, CAP, TOK), 1).astype(F32)
    pick3 = (jnp.broadcast_to(before[:, None, :], (NE, CAP, TOK)) == place).astype(F32)
    pickw = (pick3 * weight[:, None, :]).reshape(SLOTS, TOK)
    pick = pick3.reshape(SLOTS, TOK)
    sel[...] = pick
    second = (loop_ref[...] == 1).astype(F32)
    w1 = jnp.sum(pickw * second, axis=1, keepdims=True)
    w0 = jnp.sum(pickw * (1.0 - second), axis=1, keepdims=True)
    lane = lax.broadcasted_iota(jnp.int32, (SLOTS, RANK), 1)
    mbuf[:, RANK:] = jnp.where(lane >= RANK // 2, w1, w0).astype(BF16)

    def block_of(j):
        off, start, width = STEPS[j]
        return lax.rem(y + off, NY), start, width

    def fill(j):
        yj, start, width = block_of(j)
        picked = sel[...].astype(BF16)

        def one(q, c):
            at = pl.multiple_of((NY * q + yj) * ROWS + start, 128)
            dys[j][q] = dot(picked, cot[:, pl.ds(at, width)]).astype(BF16)
            return c

        lax.fori_loop(0, NX, one, 0)
        mine = pl.ds(pl.multiple_of(e * CAP, CAP), CAP)
        dyr[j][:, mine, :] = dys[j][:, mine, :]

    def blk(p):
        return pl.ds(pl.multiple_of(p * CAP, CAP), CAP)

    def z_each(make):
        def one(k, c):
            make(lax.rem(e + k, NE))
            return c

        lax.fori_loop(1, NE, one, 0)

    def dy_copy(j, p, s):
        return rcopy(
            dys[j].at[:, blk(p), :], dyr[j].at[:, blk(s), :], dy_s.at[j, p], dy_r.at[j, s], zdev(p)
        )

    def meta_copy(p, s):
        return rcopy(mbuf.at[blk(p), :], msend.at[blk(s), :], m_s.at[p], m_r.at[s], zdev(p))

    def h_copy(p, s):
        return rcopy(hx.at[s], hx.at[s], x_s.at[0, p], x_r.at[0, s], xdev(p))

    def d_copy(p, s):
        return rcopy(dx.at[s], dx.at[s], x_s.at[1, p], x_r.at[1, s], xdev(p))

    def q1_copy(p, s):
        return rcopy(q1s.at[p], q1r.at[s], x_s.at[2, p], x_r.at[2, s], xdev(p))

    def t_copy(j, p, s):
        return rcopy(tsd[j].at[p], trv[j].at[s], x_s.at[3 + j, p], x_r.at[3 + j, s], xdev(p))

    def q2_copy(p, s):
        return rcopy(q2s.at[p], q2r.at[s], y_s.at[0, p], y_r.at[0, s], ydev(p))

    def p_copy(j, p):
        return rcopy(ps.at[j], pr.at[j], y_s.at[1, j], y_r.at[1, j], ydev(p))

    def zc(n, src, dst, p, s):
        return rcopy(src.at[p], dst.at[s], z_s.at[n, p], z_r.at[n, s], zdev(p))

    def x_each(make):
        for k in range(1, NX):
            make(lax.rem(x + k, NX))

    def y_each(make):
        for k in range(1, NY):
            make(lax.rem(y + k, NY))

    loads[0].wait()
    fill(0)
    pl.semaphore_wait(barrier, NE - 1 + 2 * 3)
    z_each(lambda p: dy_copy(0, p, e).start())
    loads[1].wait()
    x_each(lambda p: h_copy(p, x).start())

    loads[2].wait()
    picked = sel[...].astype(BF16)
    p0 = dot(cot[...], aout[0]).astype(BF16)
    p1 = dot(cot[...], aout[1]).astype(BF16)
    both = jnp.where(w1 > 0.0, dot(picked, p1), dot(picked, p0))
    mbuf[:, :RANK] = both.astype(BF16)
    mine = blk(e)
    msend[mine, :] = mbuf[mine, :]
    z_each(lambda p: meta_copy(p, e).start())
    for j in range(1, NS):
        fill(j)
        z_each(lambda p: dy_copy(j, p, e).start())

    loads[3].wait()
    for p in range(NE):
        pair = jnp.concatenate(
            [ain[0, 8 * p : 8 * p + 8, :].astype(F32), ain[1, 8 * p : 8 * p + 8, :].astype(F32)], axis=0
        )
        aperm[16 * p : 16 * p + 16, :] = pair.astype(BF16)
    hid = hx[x]
    down = lax.dot_general(hid, aperm[...], (((1,), (1,)), ((), ())), preferred_element_type=F32)

    z_each(lambda s: meta_copy(s, s).wait_recv())
    mix = msend[:, RANK:].astype(F32)
    proj = msend[:, :RANK]
    wfull = mix + pltpu.roll(mix, RANK // 2, 1)
    high = jnp.where(lane >= RANK // 2, mix, 0.0)
    whigh = high + pltpu.roll(high, RANK // 2, 1)
    wlow = wfull - whigh
    mrecv[...] = wfull
    lane2 = lax.broadcasted_iota(jnp.int32, (SLOTS, EXT), 1)
    odd = jnp.bitwise_and(jnp.right_shift(lane2, 3), 1) == 1
    wsel = jnp.where(
        odd, jnp.concatenate([whigh, whigh], axis=1), jnp.concatenate([wlow, wlow], axis=1)
    )
    keep = wsel > 0.0
    dx[x] = jnp.where(keep, down, 0.0).astype(BF16)
    x_each(lambda p: d_copy(p, x).start())
    r_at = lax.broadcasted_iota(jnp.int32, (RANK, EXT), 0)
    n_at = lax.broadcasted_iota(jnp.int32, (RANK, EXT), 1)
    spread = jnp.bitwise_or(
        jnp.left_shift(jnp.right_shift(n_at, 4), 3), jnp.bitwise_and(n_at, 7)
    )
    expand = (spread == r_at).astype(F32).astype(BF16)
    wproj = (wfull * proj.astype(F32)).astype(BF16)
    wpm = jnp.where(keep, dot(wproj, expand), 0.0).astype(BF16)
    projm = jnp.where(keep, dot(proj, expand), 0.0).astype(BF16)
    acc[...] = dot(projm, aperm[...])
    qt = lax.dot_general(hid, wpm, (((0,), (0,)), ((), ())), preferred_element_type=F32)
    for p in range(NX):
        q1s[p] = qt[4 * ACOL * p : 4 * ACOL * (p + 1), :].astype(BF16)
    x_each(lambda p: q1_copy(p, x).start())

    def arrive(j):
        yj, start, width = block_of(j)
        z_each(lambda s: dy_copy(j, s, s).wait_recv())

        def one(q, c):
            wf = mrecv[...]
            if width > RANK:
                wf = jnp.concatenate([wf, wf], axis=1)
            tsd[j][q] = (dyr[j][q].astype(F32) * wf).T.astype(BF16)
            return c

        lax.fori_loop(0, NX, one, 0)
        x_each(lambda p: t_copy(j, p, x).start())
        if j == 0:
            loads[4].wait()

        def two(q, c):
            at = pl.multiple_of((NY * q + yj) * ROWS + start, 128)
            acc[...] += dot(dyr[j][q], wm[pl.ds(at, width), :])
            return c

        lax.fori_loop(0, NX, two, 0)

    def product(j):
        x_each(lambda s: t_copy(j, s, s).wait_recv())
        if j == 0:
            x_each(lambda s: h_copy(s, s).wait_recv())
            x_each(lambda s: d_copy(s, s).wait_recv())
        mine = tsd[j][x]
        main = dot(mine, hx[x])
        extra = dot(mine, dx[x])
        for k in range(1, NX):
            s = lax.rem(x + k, NX)
            main = main + dot(trv[j][s], hx[s])
            extra = extra + dot(trv[j][s], dx[s])
        return main, extra

    def reduce_y(j):
        main, extra = product(j)
        ps[j, :, :HID] = main.astype(BF16)
        ps[j, :, HID:] = extra.astype(BF16)
        p_copy(j, lax.rem(y + STEPS[j][0], NY)).start()

    arrive(0)
    x_each(lambda s: q1_copy(s, s).wait_recv())
    total = q1s[x].astype(F32)
    for k in range(1, NX):
        total = total + q1r[lax.rem(x + k, NX)].astype(F32)
    for p in range(NY):
        q2s[p] = total[ACOL * p : ACOL * (p + 1), :].astype(BF16)
    y_each(lambda p: q2_copy(p, y).start())
    reduce_y(0)

    arrive(1)
    y_each(lambda s: q2_copy(s, s).wait_recv())
    total = q2s[y].astype(F32)
    for k in range(1, NY):
        total = total + q2r[lax.rem(y + k, NY)].astype(F32)
    padded = jnp.concatenate([total, jnp.zeros((RANK - ACOL, EXT), F32)], axis=0)
    rzs[...] = padded.T.astype(BF16).reshape(NE, 16, RANK)
    z_each(lambda p: zc(0, rzs, rzr, p, e).start())
    reduce_y(1)

    arrive(2)
    z_each(lambda s: zc(0, rzs, rzr, s, s).wait_recv())
    rzr[e] = rzs[e]
    total = jnp.sum(rzr[...].astype(F32), axis=0)
    ga_ref[0] = total[:8, :ACOL]
    ga_ref[1] = total[8:, :ACOL]
    reduce_y(2)

    arrive(3)
    arrive(4)
    grad = acc[...]
    wf = mrecv[...]
    mixed = jnp.sum(hx[x].astype(F32) * grad, axis=1, keepdims=True)
    place2 = lax.broadcasted_iota(jnp.int32, (NE, CAP, RANK), 1)
    lane3 = lax.broadcasted_iota(jnp.int32, (NE, CAP, RANK), 2)
    diag = place2 == lane3
    spreadm = jnp.broadcast_to(mixed, (SLOTS, RANK)).reshape(NE, CAP, RANK)
    rows = jnp.sum(jnp.where(diag, spreadm, 0.0), axis=1)
    xs_[...] = jnp.broadcast_to(rows[:, None, :], (NE, 8, RANK))
    z_each(lambda p: zc(1, xs_, xr_, p, e).start())
    hg_ref[...] = (jnp.concatenate([wf] * (HID // RANK), axis=1) * grad).astype(BF16)

    for j in range(3, NS):
        off, start, width = STEPS[j]
        main, extra = product(j)
        if j == 3:
            for k in range(3):
                p_copy(k, k).wait_recv()
        part = slice(start, start + width)
        for k in range(3):
            main = main + pr[k, part, :HID].astype(F32)
            extra = extra + pr[k, part, HID:].astype(F32)
        dw_ref[part, :] = main
        own[part, :] = extra
    gzs[...] = own[...].T.astype(BF16).reshape(NE, 16, ROWS)
    z_each(lambda p: zc(2, gzs, gzr, p, e).start())

    z_each(lambda s: zc(1, xs_, xr_, s, s).wait_recv())
    xr_[e] = xs_[e]
    got = jnp.broadcast_to(xr_[:, 0:1, :], (NE, CAP, RANK))
    column = jnp.sum(jnp.where(diag, got, 0.0), axis=2, keepdims=True)
    per_expert = jnp.sum(sel[...].reshape(NE, CAP, TOK) * column, axis=1)
    for k in range(8):
        hit = routes_ref[k : k + 1, :] == expert_id
        cwg_ref[k : k + 1, :] = jnp.sum(jnp.where(hit, per_expert, 0.0), axis=0, keepdims=True)

    z_each(lambda s: zc(2, gzs, gzr, s, s).wait_recv())
    gzr[e] = gzs[e]
    total = jnp.sum(gzr[...].astype(F32), axis=0)
    gb_ref[0] = total[:8, :]
    gb_ref[1] = total[8:, :]

    for j in range(NS):
        z_each(lambda p: dy_copy(j, p, e).wait_send())
        x_each(lambda p: t_copy(j, p, x).wait_send())
    z_each(lambda p: meta_copy(p, e).wait_send())
    z_each(lambda p: zc(0, rzs, rzr, p, e).wait_send())
    z_each(lambda p: zc(1, xs_, xr_, p, e).wait_send())
    z_each(lambda p: zc(2, gzs, gzr, p, e).wait_send())
    x_each(lambda p: h_copy(p, x).wait_send())
    x_each(lambda p: d_copy(p, x).wait_send())
    x_each(lambda p: q1_copy(p, x).wait_send())
    y_each(lambda p: q2_copy(p, y).wait_send())
    for j in range(3):
        p_copy(j, lax.rem(y + STEPS[j][0], NY)).wait_send()


def on_device(cotangent, hidden, down_matrix, adapter_in, adapter_out, probs, routes, token_loop):
    vmem = pl.BlockSpec(memory_space=pltpu.VMEM)
    anyw = pl.BlockSpec(memory_space=pl.ANY)
    widths = [w for _, _, w in STEPS]
    scratch = [
        pltpu.VMEM((TOK, MODEL), BF16),
        pltpu.VMEM((2, MODEL, RANK), BF16),
        pltpu.VMEM((2, RANK, HID), BF16),
        pltpu.VMEM((MODEL, HID), BF16),
        pltpu.VMEM((NX, SLOTS, HID), BF16),
        pltpu.VMEM((NX, SLOTS, EXT), BF16),
        pltpu.VMEM((EXT, HID), BF16),
        pltpu.VMEM((8, RANK), F32),
        pltpu.VMEM((SLOTS, EXT), BF16),
        pltpu.VMEM((SLOTS, HID), F32),
        pltpu.VMEM((SLOTS, TOK), F32),
        pltpu.VMEM((SLOTS, EXT), BF16),
        pltpu.VMEM((SLOTS, RANK), F32),
        pltpu.VMEM((NX, 4 * ACOL, EXT), BF16),
        pltpu.VMEM((NX, 4 * ACOL, EXT), BF16),
        pltpu.VMEM((NY, ACOL, EXT), BF16),
        pltpu.VMEM((NY, ACOL, EXT), BF16),
        pltpu.VMEM((NE, 16, RANK), BF16),
        pltpu.VMEM((NE, 16, RANK), BF16),
        pltpu.VMEM((NE, 8, RANK), F32),
        pltpu.VMEM((NE, 8, RANK), F32),
        pltpu.VMEM((NE, 16, ROWS), BF16),
        pltpu.VMEM((NE, 16, ROWS), BF16),
        pltpu.VMEM((3, ROWS, HID + EXT), BF16),
        pltpu.VMEM((3, ROWS, HID + EXT), BF16),
        pltpu.VMEM((ROWS, EXT), F32),
    ]
    scratch += [pltpu.VMEM((NX, SLOTS, w), BF16) for w in widths]
    scratch += [pltpu.VMEM((NX, SLOTS, w), BF16) for w in widths]
    scratch += [pltpu.VMEM((NX, w, SLOTS), BF16) for w in widths]
    scratch += [pltpu.VMEM((NX, w, SLOTS), BF16) for w in widths]
    sem = pltpu.SemaphoreType.DMA
    scratch += [
        sem((5,)),
        sem((NS, NE)),
        sem((NS, NE)),
        sem((NE,)),
        sem((NE,)),
        sem((3 + NS, NX)),
        sem((3 + NS, NX)),
        sem((2, NY)),
        sem((2, NY)),
        sem((3, NE)),
        sem((3, NE)),
    ]
    hg, dw, cwg, ga, gb = pl.pallas_call(
        kernel,
        out_shape=(
            jax.ShapeDtypeStruct((SLOTS, HID), BF16),
            jax.ShapeDtypeStruct((ROWS, HID), F32),
            jax.ShapeDtypeStruct((8, TOK), F32),
            jax.ShapeDtypeStruct((2, 8, ACOL), F32),
            jax.ShapeDtypeStruct((2, 8, ROWS), F32),
        ),
        in_specs=[anyw] * 5 + [vmem] * 3,
        out_specs=(vmem,) * 5,
        scratch_shapes=scratch,
        compiler_params=pltpu.CompilerParams(
            collective_id=0, has_side_effects=True, vmem_limit_bytes=56 * 2**20
        ),
        name="backward",
    )(
        cotangent,
        hidden.reshape(SLOTS, HID),
        down_matrix.reshape(MODEL, HID),
        adapter_in,
        adapter_out,
        probs.T,
        routes.T,
        token_loop.reshape(1, TOK),
    )
    return (
        hg.reshape(hidden.shape),
        dw.reshape(1, ROWS, HID),
        cwg.T,
        ga,
        jnp.swapaxes(gb, 1, 2),
    )


def solution(mesh):
    return jax.shard_map(
        on_device,
        mesh=mesh,
        in_specs=(
            P(("dp", "expert"), None),
            P("dp", "expert", None, None),
            P("expert", None, None),
            P(),
            P(),
            P(("dp", "expert"), None),
            P(("dp", "expert"), None),
            P(("dp", "expert")),
        ),
        out_specs=(
            P("dp", "expert", None, None),
            P("expert", "dp", None),
            P(("dp", "expert"), None),
            P(None, "expert", "dp"),
            P(None, "dp", "expert"),
        ),
        check_vma=False,
    )
```

```python
import functools

import jax
import jax.numpy as jnp
from jax import lax
from jax.experimental import pallas as pl
from jax.experimental.pallas import tpu as pltpu
from jax.sharding import PartitionSpec as P

MESH = pl.DeviceIdType.MESH
F32 = jnp.float32
BF16 = jnp.bfloat16

NX = 4
NY = 4
NE = 16
CAP = 16
TOK = 128
SLOTS = NE * CAP
MODEL = 4096
HID = 768
RANK = 128
EXT = 2 * RANK
ROWS = MODEL // (NX * NY)
ACOL = HID // (NX * NY)

STEPS = (
    (1, 0, 256),
    (2, 0, 128),
    (2, 128, 128),
    (3, 0, 128),
    (3, 128, 128),
    (0, 0, 128),
    (0, 128, 128),
)
NS = len(STEPS)
NP = sum(1 for off, _, _ in STEPS if off)


def rcopy(src, dst, send, recv, dev):
    return pltpu.make_async_remote_copy(
        src_ref=src, dst_ref=dst, send_sem=send, recv_sem=recv, device_id=dev, device_id_type=MESH
    )


def dot(a, b):
    return jnp.dot(a, b, preferred_element_type=F32)


def dot_t(a, b):
    return lax.dot_general(a, b, (((1,), (1,)), ((), ())), preferred_element_type=F32)


def blk(p):
    return pl.ds(pl.multiple_of(p * CAP, CAP), CAP)


def kernel(cot_h, hid_h, w_h, ain_h, aout_h, probs_ref, routes_ref, loop_ref, *refs):
    hg_ref, dw_ref, cwg_ref, ga_ref, gb_ref = refs[:5]
    (cot, aout, ain, wm, hx, dx, aperm, pbuf, precv, wv, acc, sel) = refs[5:17]
    (mrow, mxr, mxs, q1s, q1r, q2s, q2r, rzs, rzr, xs, xr, gzs, gzr, ps, pr) = refs[17:32]
    dys = refs[32 : 32 + NS]
    dyr = refs[32 + NS : 32 + 2 * NS]
    tsd = refs[32 + 2 * NS : 32 + 3 * NS]
    trv = refs[32 + 3 * NS : 32 + 4 * NS]
    lsem, z_s, z_r, x_s, x_r, y_s, y_r = refs[32 + 4 * NS :]

    dp = lax.axis_index("dp")
    e = lax.axis_index("expert")
    x = dp // NY
    y = lax.rem(dp, NY)

    def zdev(p):
        return (dp, p)

    def xdev(p):
        return (p * NY + y, e)

    def ydev(p):
        return (x * NY + p, e)

    def z_each(make):
        def one(k, c):
            make(lax.rem(e + k, NE))
            return c

        lax.fori_loop(1, NE, one, 0)

    def x_each(make):
        for k in range(1, NX):
            make(lax.rem(x + k, NX))

    def y_each(make):
        for k in range(1, NY):
            make(lax.rem(y + k, NY))

    loads = [
        pltpu.make_async_copy(cot_h, cot, lsem.at[0]),
        pltpu.make_async_copy(aout_h, aout, lsem.at[2]),
        pltpu.make_async_copy(hid_h, hx.at[x], lsem.at[1]),
        pltpu.make_async_copy(ain_h, ain, lsem.at[3]),
        pltpu.make_async_copy(w_h, wm, lsem.at[4]),
    ]
    for one in loads:
        one.start()

    barrier = pltpu.get_barrier_semaphore()
    z_each(lambda p: pl.semaphore_signal(barrier, inc=1, device_id=zdev(p), device_id_type=MESH))
    x_each(lambda p: pl.semaphore_signal(barrier, inc=1, device_id=xdev(p), device_id_type=MESH))
    y_each(lambda p: pl.semaphore_signal(barrier, inc=1, device_id=ydev(p), device_id_type=MESH))

    place = lax.broadcasted_iota(jnp.int32, (NE, CAP, RANK), 1)
    lane = lax.broadcasted_iota(jnp.int32, (NE, CAP, RANK), 2)

    routes = routes_ref[...]
    probs = probs_ref[...].astype(F32)
    expert_id = lax.broadcasted_iota(jnp.int32, (NE, TOK), 0)
    named = jnp.zeros((NE, TOK), F32)
    weight = jnp.zeros((NE, TOK), F32)
    for k in range(8):
        hit = (routes[k : k + 1, :] == expert_id).astype(F32)
        named = named + hit
        weight = weight + hit * probs[k : k + 1, :]
    row = lax.broadcasted_iota(jnp.int32, (TOK, TOK), 0)
    col = lax.broadcasted_iota(jnp.int32, (TOK, TOK), 1)
    before = dot(named.astype(BF16), (row < col).astype(F32).astype(BF16))
    before = jnp.where(named > 0.5, before, -1.0)
    pick3 = (jnp.broadcast_to(before[:, None, :], (NE, CAP, TOK)) == place.astype(F32)).astype(F32)
    pickw = (pick3 * weight[:, None, :]).reshape(SLOTS, TOK)
    sel[...] = pick3.reshape(SLOTS, TOK)
    second = (loop_ref[...] == 1).astype(F32)
    w1 = jnp.sum(pickw * second, axis=1, keepdims=True)
    w0 = jnp.sum(pickw * (1.0 - second), axis=1, keepdims=True)

    def to_rows(column):
        return jnp.broadcast_to(column, (SLOTS, RANK)).reshape(NE, CAP, RANK)

    both = jnp.where(lane == place, to_rows(w0), 0.0) + jnp.where(
        lane == place + CAP, to_rows(w1), 0.0
    )
    mrow[...] = jnp.sum(both, axis=1)[:, None, :]

    def block_of(j):
        off, start, width = STEPS[j]
        return lax.rem(y + off, NY), start, width

    def fill(j):
        yj, start, width = block_of(j)
        picked = sel[...].astype(BF16)

        def one(q, c):
            at = pl.multiple_of((NY * q + yj) * ROWS + start, 128)
            dys[j][q] = dot(picked, cot[:, pl.ds(at, width)]).astype(BF16)
            return c

        lax.fori_loop(0, NX, one, 0)
        dyr[j][:, blk(e), :] = dys[j][:, blk(e), :]

    most = pl.ds(0, (NE - 1) * CAP)

    def dy_copy(j, p):
        return rcopy(dys[j].at[:, blk(p), :], dyr[j].at[:, blk(e), :], z_s.at[j], z_r.at[j], zdev(p))

    def dy_all(j):
        return rcopy(dys[j].at[:, most, :], dyr[j].at[:, most, :], z_s.at[j], z_r.at[j], zdev(e))

    def pj_copy(p):
        return rcopy(pbuf.at[blk(p), :], precv.at[blk(e), :], z_s.at[NS], z_r.at[NS], zdev(p))

    def pj_all():
        return rcopy(pbuf.at[most, :], precv.at[most, :], z_s.at[NS], z_r.at[NS], zdev(e))

    def zc(n, src, dst, p):
        return rcopy(src.at[p], dst.at[e], z_s.at[NS + n], z_r.at[NS + n], zdev(p))

    def zc_all(n, src, dst):
        part = pl.ds(0, NE - 1)
        return rcopy(src.at[part], dst.at[part], z_s.at[NS + n], z_r.at[NS + n], zdev(e))

    def xc(n, src, dst, p):
        return rcopy(src, dst, x_s.at[n], x_r.at[n], xdev(p))

    def yc(n, src, dst, p):
        return rcopy(src, dst, y_s.at[n], y_r.at[n], ydev(p))

    three = pl.ds(0, 3)

    def h_all():
        return xc(0, hx.at[three], hx.at[three], x)

    def m_all():
        return xc(1, mxr.at[three], mxr.at[three], x)

    def q1_all():
        return yc(0, q1s.at[three], q1r.at[three], y)

    def q2_all():
        return xc(2, q2s.at[three], q2r.at[three], x)

    def t_all(j):
        return xc(3 + j, tsd[j].at[three], trv[j].at[three], x)

    def p_copy(j, p):
        off, start, width = STEPS[j]
        at = (off - 1, pl.ds(start, width))
        return yc(1 + j, ps.at[at], pr.at[at], p)

    loads[0].wait()
    fill(0)
    loads[1].wait()
    picked = sel[...].astype(BF16)
    p0 = dot(cot[...], aout[0]).astype(BF16)
    p1 = dot(cot[...], aout[1]).astype(BF16)
    pbuf[...] = jnp.where(w1 > 0.0, dot(picked, p1), dot(picked, p0)).astype(BF16)
    precv[blk(e), :] = pbuf[blk(e), :]
    mxr[x, e] = mrow[e]
    fill(1)
    loads[2].wait()
    pl.semaphore_wait(barrier, NE - 1 + 2 * 3)
    z_each(lambda p: rcopy(mrow.at[p], mxr.at[x, e], z_s.at[NS + 1], z_r.at[NS + 1], zdev(p)).start())
    z_each(lambda p: pj_copy(p).start())
    z_each(lambda p: dy_copy(0, p).start())
    x_each(lambda p: xc(0, hx.at[x], hx.at[x], p).start())
    z_each(lambda p: dy_copy(1, p).start())
    for j in range(2, NS):
        fill(j)
        z_each(lambda p: dy_copy(j, p).start())

    loads[3].wait()
    for p in range(NE):
        pair = jnp.concatenate(
            [ain[0, 8 * p : 8 * p + 8, :].astype(F32), ain[1, 8 * p : 8 * p + 8, :].astype(F32)], axis=0
        )
        aperm[16 * p : 16 * p + 16, :] = pair.astype(BF16)
    hid = hx[x]

    def weights(s):
        got = jnp.broadcast_to(mxr[s], (NE, CAP, RANK))
        low = jnp.sum(jnp.where(lane == place, got, 0.0), axis=2, keepdims=True)
        high = jnp.sum(jnp.where(lane == place + CAP, got, 0.0), axis=2, keepdims=True)
        low = jnp.broadcast_to(low, (NE, CAP, RANK)).reshape(SLOTS, RANK)
        high = jnp.broadcast_to(high, (NE, CAP, RANK)).reshape(SLOTS, RANK)
        return low, high

    lane2 = lax.broadcasted_iota(jnp.int32, (SLOTS, EXT), 1)
    odd = jnp.bitwise_and(jnp.right_shift(lane2, 3), 1) == 1

    def kept(low, high):
        picked_w = jnp.where(
            odd, jnp.concatenate([high, high], axis=1), jnp.concatenate([low, low], axis=1)
        )
        return picked_w > 0.0

    part = pl.ds(0, NE - 1)
    rcopy(mrow.at[part], mxr.at[x, part], z_s.at[NS + 1], z_r.at[NS + 1], zdev(e)).wait_recv()
    x_each(lambda p: xc(1, mxr.at[x], mxr.at[x], p).start())
    low, high = weights(x)
    wfull = low + high
    wv[...] = wfull
    keep = kept(low, high)
    pj_all().wait_recv()
    proj = precv[...]
    r_at = lax.broadcasted_iota(jnp.int32, (RANK, EXT), 0)
    n_at = lax.broadcasted_iota(jnp.int32, (RANK, EXT), 1)
    spread = jnp.bitwise_or(
        jnp.left_shift(jnp.right_shift(n_at, 4), 3), jnp.bitwise_and(n_at, 7)
    )
    expand = (spread == r_at).astype(F32).astype(BF16)
    wproj = (wfull * proj.astype(F32)).astype(BF16)
    wpm = jnp.where(keep, dot(wproj, expand), 0.0).astype(BF16)
    projm = jnp.where(keep, dot(proj, expand), 0.0).astype(BF16)
    acc[...] = dot(projm, aperm[...])
    qt = lax.dot_general(hid, wpm, (((0,), (0,)), ((), ())), preferred_element_type=F32)
    for d in range(NX * NY):
        q1s[d % NY, d // NY] = qt[ACOL * d : ACOL * (d + 1), :].astype(BF16)
    y_each(lambda p: yc(0, q1s.at[p], q1r.at[y], p).start())

    def arrive(j):
        yj, start, width = block_of(j)
        dy_all(j).wait_recv()

        def one(q, c):
            wf = wv[...]
            if width > RANK:
                wf = jnp.concatenate([wf, wf], axis=1)
            tsd[j][q] = (dyr[j][q].astype(F32) * wf).T.astype(BF16)
            return c

        lax.fori_loop(0, NX, one, 0)
        x_each(lambda p: xc(3 + j, tsd[j].at[p], trv[j].at[x], p).start())
        if j == 0:
            loads[4].wait()

        def two(q, c):
            at = pl.multiple_of((NY * q + yj) * ROWS + start, 128)
            acc[...] += dot(dyr[j][q], wm[pl.ds(at, width), :])
            return c

        lax.fori_loop(0, NX, two, 0)

    def product(j):
        t_all(j).wait_recv()
        mine = tsd[j][x]
        main = dot(mine, hx[x])
        extra = dot(mine, dx[x])
        for k in range(1, NX):
            s = lax.rem(x + k, NX)
            main = main + dot(trv[j][s], hx[s])
            extra = extra + dot(trv[j][s], dx[s])
        return main, extra

    def reduce_y(j):
        off, start, width = STEPS[j]
        main, extra = product(j)
        ps[off - 1, start : start + width, :HID] = main.astype(BF16)
        ps[off - 1, start : start + width, HID:] = extra.astype(BF16)
        p_copy(j, lax.rem(y + off, NY)).start()

    def finish_block(j):
        off, start, width = STEPS[j]
        main, extra = product(j)
        for i in range(NP):
            if STEPS[i][2] > width or STEPS[i][1] == start:
                if not (STEPS[i][2] > width and start > 0):
                    p_copy(i, y).wait_recv()
        rows = slice(start, start + width)
        for k in range(3):
            main = main + pr[k, rows, :HID].astype(F32)
            extra = extra + pr[k, rows, HID:].astype(F32)
        dw_ref[rows, :] = main
        h = start // width
        gzs[h] = extra.T.astype(BF16).reshape(NE, 16, width)
        z_each(lambda p: zc(4 + h, gzs.at[h], gzr.at[h], p).start())

    q1_all().wait_recv()
    total = q1s[y].astype(F32)
    for k in range(1, NY):
        total = total + q1r[lax.rem(y + k, NY)].astype(F32)
    q2s[...] = total.astype(BF16)
    x_each(lambda p: xc(2, q2s.at[p], q2r.at[x], p).start())

    arrive(0)
    h_all().wait_recv()
    m_all().wait_recv()
    for k in range(NX):
        s = lax.rem(x + k, NX)
        low, high = weights(s)
        dx[s] = jnp.where(kept(low, high), dot_t(hx[s], aperm[...]), 0.0).astype(BF16)
    arrive(1)
    reduce_y(0)
    arrive(2)
    q2_all().wait_recv()
    total = q2s[x].astype(F32)
    for k in range(1, NX):
        total = total + q2r[lax.rem(x + k, NX)].astype(F32)
    padded = jnp.concatenate([total, jnp.zeros((RANK - ACOL, EXT), F32)], axis=0)
    rzs[...] = padded.T.astype(BF16).reshape(NE, 16, RANK)
    z_each(lambda p: zc(2, rzs, rzr, p).start())
    reduce_y(1)
    arrive(3)
    reduce_y(2)
    arrive(4)
    reduce_y(3)
    arrive(5)
    reduce_y(4)
    arrive(6)

    grad = acc[...]
    mixed = jnp.sum(hx[x].astype(F32) * grad, axis=1, keepdims=True)
    xs[...] = jnp.sum(jnp.where(lane == place, to_rows(mixed), 0.0), axis=1)[:, None, :]
    z_each(lambda p: zc(3, xs, xr, p).start())
    hg_ref[...] = (jnp.concatenate([wv[...]] * (HID // RANK), axis=1) * grad).astype(BF16)

    finish_block(5)

    zc_all(2, rzs, rzr).wait_recv()
    rzr[e] = rzs[e]
    total = jnp.sum(rzr[...].astype(F32), axis=0)
    ga_ref[0] = total[:8, :ACOL]
    ga_ref[1] = total[8:, :ACOL]

    finish_block(6)

    zc_all(3, xs, xr).wait_recv()
    xr[e] = xs[e]
    got = jnp.broadcast_to(xr[...], (NE, CAP, RANK))
    column = jnp.sum(jnp.where(lane == place, got, 0.0), axis=2, keepdims=True)
    per_expert = jnp.sum(sel[...].reshape(NE, CAP, TOK) * column, axis=1)
    for k in range(8):
        hit = routes_ref[k : k + 1, :] == expert_id
        cwg_ref[k : k + 1, :] = jnp.sum(jnp.where(hit, per_expert, 0.0), axis=0, keepdims=True)

    rcopy(mrow.at[part], mxr.at[x, part], z_s.at[NS + 1], z_r.at[NS + 1], zdev(e)).wait_send()
    pj_all().wait_send()
    for j in range(NS):
        dy_all(j).wait_send()
        t_all(j).wait_send()
    h_all().wait_send()
    m_all().wait_send()
    q1_all().wait_send()
    q2_all().wait_send()
    zc_all(2, rzs, rzr).wait_send()
    zc_all(3, xs, xr).wait_send()
    for j in range(NP):
        p_copy(j, y).wait_send()

    for h in range(2):
        zc_all(4 + h, gzs.at[h], gzr.at[h]).wait_recv()
        gzr[h, e] = gzs[h, e]
        total = jnp.sum(gzr[h].astype(F32), axis=0)
        half = slice(h * ROWS // 2, (h + 1) * ROWS // 2)
        gb_ref[0, :, half] = total[:8, :]
        gb_ref[1, :, half] = total[8:, :]
    for h in range(2):
        zc_all(4 + h, gzs.at[h], gzr.at[h]).wait_send()


def store_kernel(*refs):
    ins, outs, sem = refs[:5], refs[5:10], refs[10]
    moves = [pltpu.make_async_copy(a, b, sem.at[n]) for n, (a, b) in enumerate(zip(ins, outs))]
    for one in moves:
        one.start()
    for one in moves:
        one.wait()


def on_device(cotangent, hidden, down_matrix, adapter_in, adapter_out, probs, routes, token_loop):
    vmem = pl.BlockSpec(memory_space=pltpu.VMEM)
    anyw = pl.BlockSpec(memory_space=pl.ANY)
    hbm = pl.BlockSpec(memory_space=pltpu.HBM)
    widths = [w for _, _, w in STEPS]
    scratch = [
        pltpu.VMEM((TOK, MODEL), BF16),
        pltpu.VMEM((2, MODEL, RANK), BF16),
        pltpu.VMEM((2, RANK, HID), BF16),
        pltpu.VMEM((MODEL, HID), BF16),
        pltpu.VMEM((NX, SLOTS, HID), BF16),
        pltpu.VMEM((NX, SLOTS, EXT), BF16),
        pltpu.VMEM((EXT, HID), BF16),
        pltpu.VMEM((SLOTS, RANK), BF16),
        pltpu.VMEM((SLOTS, RANK), BF16),
        pltpu.VMEM((SLOTS, RANK), F32),
        pltpu.VMEM((SLOTS, HID), F32),
        pltpu.VMEM((SLOTS, TOK), F32),
        pltpu.VMEM((NE, 1, RANK), F32),
        pltpu.VMEM((NX, NE, 1, RANK), F32),
        pltpu.VMEM((8, RANK), F32),
        pltpu.VMEM((NY, NX, ACOL, EXT), BF16),
        pltpu.VMEM((NY, NX, ACOL, EXT), BF16),
        pltpu.VMEM((NX, ACOL, EXT), BF16),
        pltpu.VMEM((NX, ACOL, EXT), BF16),
        pltpu.VMEM((NE, 16, RANK), BF16),
        pltpu.VMEM((NE, 16, RANK), BF16),
        pltpu.VMEM((NE, 1, RANK), F32),
        pltpu.VMEM((NE, 1, RANK), F32),
        pltpu.VMEM((2, NE, 16, ROWS // 2), BF16),
        pltpu.VMEM((2, NE, 16, ROWS // 2), BF16),
        pltpu.VMEM((3, ROWS, HID + EXT), BF16),
        pltpu.VMEM((3, ROWS, HID + EXT), BF16),
    ]
    scratch += [pltpu.VMEM((NX, SLOTS, w), BF16) for w in widths]
    scratch += [pltpu.VMEM((NX, SLOTS, w), BF16) for w in widths]
    scratch += [pltpu.VMEM((NX, w, SLOTS), BF16) for w in widths]
    scratch += [pltpu.VMEM((NX, w, SLOTS), BF16) for w in widths]
    sem = pltpu.SemaphoreType.DMA
    scratch += [
        sem((5,)),
        sem((NS + 6,)),
        sem((NS + 6,)),
        sem((3 + NS,)),
        sem((3 + NS,)),
        sem((1 + NP,)),
        sem((1 + NP,)),
    ]
    shapes = (
        ((SLOTS, HID), BF16),
        ((ROWS, HID), F32),
        ((8, TOK), F32),
        ((2, 8, ACOL), F32),
        ((2, 8, ROWS), F32),
    )
    outs = pl.pallas_call(
        kernel,
        out_shape=tuple(pltpu.VMEM(s, t) for s, t in shapes),
        in_specs=[hbm] * 5 + [vmem] * 3,
        out_specs=(vmem,) * 5,
        scratch_shapes=scratch,
        compiler_params=pltpu.CompilerParams(
            collective_id=0, has_side_effects=True, vmem_limit_bytes=56 * 2**20
        ),
        name="backward",
    )(
        cotangent,
        hidden.reshape(SLOTS, HID),
        down_matrix.reshape(MODEL, HID),
        adapter_in,
        adapter_out,
        probs.T,
        routes.T,
        token_loop.reshape(1, TOK),
    )
    hg, dw, cwg, ga, gb = pl.pallas_call(
        store_kernel,
        out_shape=tuple(jax.ShapeDtypeStruct(s, t) for s, t in shapes),
        in_specs=[vmem] * 5,
        out_specs=(anyw,) * 5,
        scratch_shapes=[sem((5,))],
        compiler_params=pltpu.CompilerParams(vmem_limit_bytes=4 * 2**20),
        name="store",
    )(*outs)
    return (
        hg.reshape(hidden.shape),
        dw.reshape(1, ROWS, HID),
        cwg.T,
        ga,
        jnp.swapaxes(gb, 1, 2),
    )


def solution(mesh):
    return jax.shard_map(
        on_device,
        mesh=mesh,
        in_specs=(
            P(("dp", "expert"), None),
            P("dp", "expert", None, None),
            P("expert", None, None),
            P(),
            P(),
            P(("dp", "expert"), None),
            P(("dp", "expert"), None),
            P(("dp", "expert")),
        ),
        out_specs=(
            P("dp", "expert", None, None),
            P("expert", "dp", None),
            P(("dp", "expert"), None),
            P(None, "expert", "dp"),
            P(None, "dp", "expert"),
        ),
        check_vma=False,
    )
```

```python
import functools

import jax
import jax.numpy as jnp
from jax import lax
from jax.experimental import pallas as pl
from jax.experimental.pallas import tpu as pltpu
from jax.sharding import PartitionSpec as P

MESH = pl.DeviceIdType.MESH
F32 = jnp.float32
BF16 = jnp.bfloat16

NX = 4
NY = 4
NE = 16
CAP = 16
TOK = 128
SLOTS = NE * CAP
MODEL = 4096
HID = 768
RANK = 128
EXT = 2 * RANK
ROWS = MODEL // (NX * NY)
ACOL = HID // (NX * NY)

ALL = (4, 1, 1)
STEPS = (
    (2, ALL, 0, 128),
    (2, ALL, 128, 128),
    (1, ALL, 0, 128),
    (3, ALL, 0, 128),
    (1, ALL, 128, 128),
    (3, ALL, 128, 128),
    (0, (3, 1, 1), 0, 128),
    (0, (1, 0, 2), 128, 128),
    (0, (2, 2, 1), 128, 128),
    (0, (1, 0, 0), 0, 128),
    (0, (1, 0, 0), 128, 128),
)
NS = len(STEPS)
NP = sum(1 for step in STEPS if step[0])
HALF = ROWS // 2


def rcopy(src, dst, send, recv, dev):
    return pltpu.make_async_remote_copy(
        src_ref=src, dst_ref=dst, send_sem=send, recv_sem=recv, device_id=dev, device_id_type=MESH
    )


def dot(a, b):
    return jnp.dot(a, b, preferred_element_type=F32)


def dot_t(a, b):
    return lax.dot_general(a, b, (((1,), (1,)), ((), ())), preferred_element_type=F32)


def owner_offset(j, q):
    _, a, b = STEPS[j][1]
    return (a * q + b) % NX


def sent_blocks(j):
    count = STEPS[j][1][0]
    return sum(1 for q in range(count) if owner_offset(j, q))


def blk(p):
    return pl.ds(pl.multiple_of(p * CAP, CAP), CAP)


def kernel(cot_h, hid_h, w_h, ain_h, aout_h, probs_h, routes_h, loop_h, *refs):
    hg_ref, dw_ref, cwg_ref, ga_ref, gb_ref = refs[:5]
    (cot, aout, ain, wm, hx, dx, aperm, pbuf, precv, wv, acc, sel) = refs[5:17]
    probs_ref, routes_ref, loop_ref = refs[17:20]
    refs = refs[3:]
    (mrow, mxr, mxs, q1s, q1r, q2s, q2r, rzs, rzr, xs, xr, gzs, gzr, ps, pr) = refs[17:32]
    dys = refs[32 : 32 + NS]
    dyr = refs[32 + NS : 32 + 2 * NS]
    tsd = refs[32 + 2 * NS : 32 + 3 * NS]
    trv = refs[32 + 3 * NS : 32 + 4 * NS]
    lsem, z_s, z_r, x_s, x_r, y_s, y_r = refs[32 + 4 * NS :]

    dp = lax.axis_index("dp")
    e = lax.axis_index("expert")
    x = dp // NY
    y = lax.rem(dp, NY)

    def zdev(p):
        return (dp, p)

    def xdev(p):
        return (p * NY + y, e)

    def ydev(p):
        return (x * NY + p, e)

    def z_each(make):
        def one(k, c):
            make(lax.rem(e + k, NE))
            return c

        lax.fori_loop(1, NE, one, 0)

    def x_each(make):
        for k in range(1, NX):
            make(lax.rem(x + k, NX))

    def y_each(make):
        for k in range(1, NY):
            make(lax.rem(y + k, NY))

    barrier = pltpu.get_barrier_semaphore()
    z_each(lambda p: pl.semaphore_signal(barrier, inc=1, device_id=zdev(p), device_id_type=MESH))
    x_each(lambda p: pl.semaphore_signal(barrier, inc=1, device_id=xdev(p), device_id_type=MESH))
    y_each(lambda p: pl.semaphore_signal(barrier, inc=1, device_id=ydev(p), device_id_type=MESH))

    small = [
        pltpu.make_async_copy(routes_h, routes_ref, lsem.at[5]),
        pltpu.make_async_copy(probs_h, probs_ref, lsem.at[6]),
        pltpu.make_async_copy(loop_h, loop_ref, lsem.at[7]),
    ]
    loads = [
        pltpu.make_async_copy(cot_h, cot, lsem.at[0]),
        pltpu.make_async_copy(aout_h, aout, lsem.at[2]),
        pltpu.make_async_copy(hid_h, hx.at[x], lsem.at[1]),
        pltpu.make_async_copy(ain_h, ain, lsem.at[3]),
        pltpu.make_async_copy(w_h, wm, lsem.at[4]),
    ]
    for one in small + loads:
        one.start()
    for one in small:
        one.wait()

    place = lax.broadcasted_iota(jnp.int32, (NE, CAP, RANK), 1)
    lane = lax.broadcasted_iota(jnp.int32, (NE, CAP, RANK), 2)

    routes = routes_ref[...]
    probs = probs_ref[...].astype(F32)
    expert_id = lax.broadcasted_iota(jnp.int32, (NE, TOK), 0)
    named = jnp.zeros((NE, TOK), F32)
    weight = jnp.zeros((NE, TOK), F32)
    for k in range(8):
        hit = (routes[k : k + 1, :] == expert_id).astype(F32)
        named = named + hit
        weight = weight + hit * probs[k : k + 1, :]
    row = lax.broadcasted_iota(jnp.int32, (TOK, TOK), 0)
    col = lax.broadcasted_iota(jnp.int32, (TOK, TOK), 1)
    before = dot(named.astype(BF16), (row < col).astype(F32).astype(BF16))
    before = jnp.where(named > 0.5, before, -1.0)
    pick3 = (jnp.broadcast_to(before[:, None, :], (NE, CAP, TOK)) == place.astype(F32)).astype(F32)
    pickw = (pick3 * weight[:, None, :]).reshape(SLOTS, TOK)
    sel[...] = pick3.reshape(SLOTS, TOK)
    second = (loop_ref[...] == 1).astype(F32)
    w1 = jnp.sum(pickw * second, axis=1, keepdims=True)
    w0 = jnp.sum(pickw * (1.0 - second), axis=1, keepdims=True)

    def to_rows(column):
        return jnp.broadcast_to(column, (SLOTS, RANK)).reshape(NE, CAP, RANK)

    both = jnp.where(lane == place, to_rows(w0), 0.0) + jnp.where(
        lane == place + CAP, to_rows(w1), 0.0
    )
    mrow[...] = jnp.sum(both, axis=1)[:, None, :]

    def column(j, q):
        off, (_, a, b), start, _ = STEPS[j]
        owner = NY * lax.rem(x + a * q + b, NX) + lax.rem(y + off, NY)
        return pl.multiple_of(owner * ROWS + start, 128)

    def fill(j):
        picked = sel[...].astype(BF16)

        def one(q, c):
            dys[j][q] = dot(picked, cot[:, pl.ds(column(j, q), STEPS[j][3])]).astype(BF16)
            return c

        lax.fori_loop(0, STEPS[j][1][0], one, 0)
        dyr[j][:, blk(e), :] = dys[j][:, blk(e), :]

    most = pl.ds(0, (NE - 1) * CAP)

    def dy_copy(j, p):
        return rcopy(dys[j].at[:, blk(p), :], dyr[j].at[:, blk(e), :], z_s.at[j], z_r.at[j], zdev(p))

    def dy_all(j):
        return rcopy(dys[j].at[:, most, :], dyr[j].at[:, most, :], z_s.at[j], z_r.at[j], zdev(e))

    def pj_copy(p):
        return rcopy(pbuf.at[blk(p), :], precv.at[blk(e), :], z_s.at[NS], z_r.at[NS], zdev(p))

    def pj_all():
        return rcopy(pbuf.at[most, :], precv.at[most, :], z_s.at[NS], z_r.at[NS], zdev(e))

    def zc(n, src, dst, p):
        return rcopy(src.at[p], dst.at[e], z_s.at[NS + n], z_r.at[NS + n], zdev(p))

    def zc_all(n, src, dst):
        part = pl.ds(0, NE - 1)
        return rcopy(src.at[part], dst.at[part], z_s.at[NS + n], z_r.at[NS + n], zdev(e))

    def xc(n, src, dst, p):
        return rcopy(src, dst, x_s.at[n], x_r.at[n], xdev(p))

    def yc(n, src, dst, p):
        return rcopy(src, dst, y_s.at[n], y_r.at[n], ydev(p))

    three = pl.ds(0, 3)

    def h_all():
        return xc(0, hx.at[three], hx.at[three], x)

    def m_all():
        return xc(1, mxr.at[three], mxr.at[three], x)

    def q1_all():
        return yc(0, q1s.at[three], q1r.at[three], y)

    def q2_all():
        return xc(2, q2s.at[three], q2r.at[three], x)

    def t_copy(j, q):
        return xc(3 + j, tsd[j].at[q], trv[j].at[q], lax.rem(x + owner_offset(j, q), NX))

    def t_all(j):
        part = pl.ds(0, sent_blocks(j))
        return xc(3 + j, tsd[j].at[part], trv[j].at[part], x)

    def p_copy(j, p):
        off, _, start, width = STEPS[j]
        at = (off - 1, pl.ds(start, width))
        return yc(1 + j, ps.at[at], pr.at[at], p)

    loads[0].wait()
    fill(0)
    loads[1].wait()
    picked = sel[...].astype(BF16)
    p0 = dot(cot[...], aout[0]).astype(BF16)
    p1 = dot(cot[...], aout[1]).astype(BF16)
    pbuf[...] = jnp.where(w1 > 0.0, dot(picked, p1), dot(picked, p0)).astype(BF16)
    precv[blk(e), :] = pbuf[blk(e), :]
    mxr[x, e] = mrow[e]
    fill(1)
    fill(2)
    loads[2].wait()
    pl.semaphore_wait(barrier, NE - 1 + 2 * 3)
    z_each(lambda p: rcopy(mrow.at[p], mxr.at[x, e], z_s.at[NS + 1], z_r.at[NS + 1], zdev(p)).start())
    z_each(lambda p: pj_copy(p).start())
    z_each(lambda p: dy_copy(0, p).start())
    x_each(lambda p: xc(0, hx.at[x], hx.at[x], p).start())
    z_each(lambda p: dy_copy(1, p).start())
    z_each(lambda p: dy_copy(2, p).start())
    for j in range(3, NS):
        fill(j)
        z_each(lambda p: dy_copy(j, p).start())

    loads[3].wait()
    for p in range(NE):
        pair = jnp.concatenate(
            [ain[0, 8 * p : 8 * p + 8, :].astype(F32), ain[1, 8 * p : 8 * p + 8, :].astype(F32)], axis=0
        )
        aperm[16 * p : 16 * p + 16, :] = pair.astype(BF16)
    hid = hx[x]

    def weights(s):
        got = jnp.broadcast_to(mxr[s], (NE, CAP, RANK))
        low = jnp.sum(jnp.where(lane == place, got, 0.0), axis=2, keepdims=True)
        high = jnp.sum(jnp.where(lane == place + CAP, got, 0.0), axis=2, keepdims=True)
        low = jnp.broadcast_to(low, (NE, CAP, RANK)).reshape(SLOTS, RANK)
        high = jnp.broadcast_to(high, (NE, CAP, RANK)).reshape(SLOTS, RANK)
        return low, high

    lane2 = lax.broadcasted_iota(jnp.int32, (SLOTS, EXT), 1)
    odd = jnp.bitwise_and(jnp.right_shift(lane2, 3), 1) == 1

    def kept(low, high):
        picked_w = jnp.where(
            odd, jnp.concatenate([high, high], axis=1), jnp.concatenate([low, low], axis=1)
        )
        return picked_w > 0.0

    part = pl.ds(0, NE - 1)
    rcopy(mrow.at[part], mxr.at[x, part], z_s.at[NS + 1], z_r.at[NS + 1], zdev(e)).wait_recv()
    x_each(lambda p: xc(1, mxr.at[x], mxr.at[x], p).start())
    low, high = weights(x)
    wfull = low + high
    wv[...] = wfull
    keep = kept(low, high)
    pj_all().wait_recv()
    proj = precv[...]
    r_at = lax.broadcasted_iota(jnp.int32, (RANK, EXT), 0)
    n_at = lax.broadcasted_iota(jnp.int32, (RANK, EXT), 1)
    spread = jnp.bitwise_or(
        jnp.left_shift(jnp.right_shift(n_at, 4), 3), jnp.bitwise_and(n_at, 7)
    )
    expand = (spread == r_at).astype(F32).astype(BF16)
    wproj = (wfull * proj.astype(F32)).astype(BF16)
    wpm = jnp.where(keep, dot(wproj, expand), 0.0).astype(BF16)
    projm = jnp.where(keep, dot(proj, expand), 0.0).astype(BF16)
    acc[...] = dot(projm, aperm[...])
    qt = lax.dot_general(hid, wpm, (((0,), (0,)), ((), ())), preferred_element_type=F32)
    for d in range(NX * NY):
        q1s[d % NY, d // NY] = qt[ACOL * d : ACOL * (d + 1), :].astype(BF16)
    y_each(lambda p: yc(0, q1s.at[p], q1r.at[y], p).start())

    def arrive(j):
        count, width = STEPS[j][1][0], STEPS[j][3]
        dy_all(j).wait_recv()

        def one(q, c):
            tsd[j][q] = (dyr[j][q].astype(F32) * wv[...]).T.astype(BF16)
            return c

        lax.fori_loop(0, count, one, 0)
        for q in range(sent_blocks(j)):
            t_copy(j, q).start()
        if j == 0:
            loads[4].wait()

        def two(q, c):
            acc[...] += dot(dyr[j][q], wm[pl.ds(column(j, q), width), :])
            return c

        lax.fori_loop(0, count, two, 0)

    def product(j, sums=None):
        if sent_blocks(j):
            t_all(j).wait_recv()
        for q in range(STEPS[j][1][0]):
            back = owner_offset(j, q)
            block = trv[j][q] if back else tsd[j][q]
            s = lax.rem(x + NX - back, NX)
            main, extra = dot(block, hx[s]), dot(block, dx[s])
            sums = (main, extra) if sums is None else (sums[0] + main, sums[1] + extra)
        return sums

    def reduce_y(j):
        off, _, start, width = STEPS[j]
        main, extra = product(j)
        ps[off - 1, start : start + width, :HID] = main.astype(BF16)
        ps[off - 1, start : start + width, HID:] = extra.astype(BF16)
        p_copy(j, lax.rem(y + off, NY)).start()

    def finish_half(h):
        start = h * HALF
        sums = None
        for j in range(NS):
            if STEPS[j][0] == 0 and STEPS[j][2] == start:
                sums = product(j, sums)
        main, extra = sums
        for j in range(NP):
            if STEPS[j][2] == start:
                p_copy(j, y).wait_recv()
        rows = slice(start, start + HALF)
        for k in range(3):
            main = main + pr[k, rows, :HID].astype(F32)
            extra = extra + pr[k, rows, HID:].astype(F32)
        gzs[h] = extra.T.astype(BF16).reshape(NE, 16, HALF)
        z_each(lambda p: zc(4 + h, gzs.at[h], gzr.at[h], p).start())
        dw_ref[rows, :] = main

    arrive(0)
    q1_all().wait_recv()
    total = q1s[y].astype(F32)
    for k in range(1, NY):
        total = total + q1r[lax.rem(y + k, NY)].astype(F32)
    q2s[...] = total.astype(BF16)
    x_each(lambda p: xc(2, q2s.at[p], q2r.at[x], p).start())
    arrive(1)
    arrive(2)
    h_all().wait_recv()
    m_all().wait_recv()
    for k in range(NX):
        s = lax.rem(x + k, NX)
        low, high = weights(s)
        dx[s] = jnp.where(kept(low, high), dot_t(hx[s], aperm[...]), 0.0).astype(BF16)
    reduce_y(0)
    reduce_y(1)
    arrive(3)
    q2_all().wait_recv()
    total = q2s[x].astype(F32)
    for k in range(1, NX):
        total = total + q2r[lax.rem(x + k, NX)].astype(F32)
    padded = jnp.concatenate([total, jnp.zeros((RANK - ACOL, EXT), F32)], axis=0)
    halves = padded.T.reshape(NE, 2, 8, RANK)
    rzs[...] = (halves[:, 0] + pltpu.roll(halves[:, 1], ACOL, 2)).astype(BF16)
    z_each(lambda p: zc(2, rzs, rzr, p).start())
    reduce_y(2)
    arrive(4)
    reduce_y(3)
    arrive(5)
    reduce_y(4)
    arrive(6)
    reduce_y(5)
    arrive(7)
    arrive(8)
    arrive(9)
    finish_half(0)
    arrive(10)

    grad = acc[...]
    mixed = jnp.sum(hx[x].astype(F32) * grad, axis=1, keepdims=True)
    xs[...] = jnp.sum(jnp.where(lane == place, to_rows(mixed), 0.0), axis=1)[:, None, :]
    z_each(lambda p: zc(3, xs, xr, p).start())
    finish_half(1)
    hg_ref[...] = (jnp.concatenate([wv[...]] * (HID // RANK), axis=1) * acc[...]).astype(BF16)

    zc_all(2, rzs, rzr).wait_recv()
    rzr[e] = rzs[e]
    total = jnp.sum(rzr[...].astype(F32), axis=0)
    ga_ref[0] = total[:, :ACOL]
    ga_ref[1] = total[:, ACOL : 2 * ACOL]

    zc_all(3, xs, xr).wait_recv()
    xr[e] = xs[e]
    got = jnp.broadcast_to(xr[...], (NE, CAP, RANK))
    column = jnp.sum(jnp.where(lane == place, got, 0.0), axis=2, keepdims=True)
    per_expert = jnp.sum(sel[...].reshape(NE, CAP, TOK) * column, axis=1)
    for k in range(8):
        hit = routes_ref[k : k + 1, :] == expert_id
        cwg_ref[k : k + 1, :] = jnp.sum(jnp.where(hit, per_expert, 0.0), axis=0, keepdims=True)

    rcopy(mrow.at[part], mxr.at[x, part], z_s.at[NS + 1], z_r.at[NS + 1], zdev(e)).wait_send()
    pj_all().wait_send()
    for j in range(NS):
        dy_all(j).wait_send()
        if sent_blocks(j):
            t_all(j).wait_send()
    h_all().wait_send()
    m_all().wait_send()
    q1_all().wait_send()
    q2_all().wait_send()
    zc_all(2, rzs, rzr).wait_send()
    zc_all(3, xs, xr).wait_send()
    for j in range(NP):
        p_copy(j, y).wait_send()

    for h in range(2):
        zc_all(4 + h, gzs.at[h], gzr.at[h]).wait_recv()
        gzr[h, e] = gzs[h, e]
        total = jnp.sum(gzr[h].astype(F32), axis=0)
        half = slice(h * ROWS // 2, (h + 1) * ROWS // 2)
        gb_ref[0, :, half] = total[:8, :]
        gb_ref[1, :, half] = total[8:, :]
    for h in range(2):
        zc_all(4 + h, gzs.at[h], gzr.at[h]).wait_send()


def store_kernel(*refs):
    ins, outs, sem = refs[:5], refs[5:10], refs[10]
    moves = [pltpu.make_async_copy(a, b, sem.at[n]) for n, (a, b) in enumerate(zip(ins, outs))]
    for one in moves:
        one.start()
    for one in moves:
        one.wait()


def on_device(cotangent, hidden, down_matrix, adapter_in, adapter_out, probs, routes, token_loop):
    vmem = pl.BlockSpec(memory_space=pltpu.VMEM)
    anyw = pl.BlockSpec(memory_space=pl.ANY)
    hbm = pl.BlockSpec(memory_space=pltpu.HBM)
    dims = [(blocks[0], width) for _, blocks, _, width in STEPS]
    scratch = [
        pltpu.VMEM((TOK, MODEL), BF16),
        pltpu.VMEM((2, MODEL, RANK), BF16),
        pltpu.VMEM((2, RANK, HID), BF16),
        pltpu.VMEM((MODEL, HID), BF16),
        pltpu.VMEM((NX, SLOTS, HID), BF16),
        pltpu.VMEM((NX, SLOTS, EXT), BF16),
        pltpu.VMEM((EXT, HID), BF16),
        pltpu.VMEM((SLOTS, RANK), BF16),
        pltpu.VMEM((SLOTS, RANK), BF16),
        pltpu.VMEM((SLOTS, RANK), F32),
        pltpu.VMEM((SLOTS, HID), F32),
        pltpu.VMEM((SLOTS, TOK), F32),
        pltpu.VMEM((8, TOK), BF16),
        pltpu.VMEM((8, TOK), jnp.int32),
        pltpu.VMEM((1, TOK), jnp.int32),
        pltpu.VMEM((NE, 1, RANK), F32),
        pltpu.VMEM((NX, NE, 1, RANK), F32),
        pltpu.VMEM((8, RANK), F32),
        pltpu.VMEM((NY, NX, ACOL, EXT), BF16),
        pltpu.VMEM((NY, NX, ACOL, EXT), BF16),
        pltpu.VMEM((NX, ACOL, EXT), BF16),
        pltpu.VMEM((NX, ACOL, EXT), BF16),
        pltpu.VMEM((NE, 8, RANK), BF16),
        pltpu.VMEM((NE, 8, RANK), BF16),
        pltpu.VMEM((NE, 1, RANK), F32),
        pltpu.VMEM((NE, 1, RANK), F32),
        pltpu.VMEM((2, NE, 16, ROWS // 2), BF16),
        pltpu.VMEM((2, NE, 16, ROWS // 2), BF16),
        pltpu.VMEM((3, ROWS, HID + EXT), BF16),
        pltpu.VMEM((3, ROWS, HID + EXT), BF16),
    ]
    scratch += [pltpu.VMEM((n, SLOTS, w), BF16) for n, w in dims]
    scratch += [pltpu.VMEM((n, SLOTS, w), BF16) for n, w in dims]
    scratch += [pltpu.VMEM((n, w, SLOTS), BF16) for n, w in dims]
    scratch += [pltpu.VMEM((n, w, SLOTS), BF16) for n, w in dims]
    sem = pltpu.SemaphoreType.DMA
    scratch += [
        sem((8,)),
        sem((NS + 6,)),
        sem((NS + 6,)),
        sem((3 + NS,)),
        sem((3 + NS,)),
        sem((1 + NP,)),
        sem((1 + NP,)),
    ]
    shapes = (
        ((SLOTS, HID), BF16),
        ((ROWS, HID), F32),
        ((8, TOK), F32),
        ((2, 8, ACOL), F32),
        ((2, 8, ROWS), F32),
    )
    outs = pl.pallas_call(
        kernel,
        out_shape=tuple(pltpu.VMEM(s, t) for s, t in shapes),
        in_specs=[hbm] * 8,
        out_specs=(vmem,) * 5,
        scratch_shapes=scratch,
        compiler_params=pltpu.CompilerParams(
            collective_id=0, has_side_effects=True, vmem_limit_bytes=56 * 2**20
        ),
        name="backward",
    )(
        cotangent,
        hidden.reshape(SLOTS, HID),
        down_matrix.reshape(MODEL, HID),
        adapter_in,
        adapter_out,
        probs.T,
        routes.T,
        token_loop.reshape(1, TOK),
    )
    hg, dw, cwg, ga, gb = pl.pallas_call(
        store_kernel,
        out_shape=tuple(jax.ShapeDtypeStruct(s, t) for s, t in shapes),
        in_specs=[vmem] * 5,
        out_specs=(anyw,) * 5,
        scratch_shapes=[sem((5,))],
        compiler_params=pltpu.CompilerParams(vmem_limit_bytes=4 * 2**20),
        name="store",
    )(*outs)
    return (
        hg.reshape(hidden.shape),
        dw.reshape(1, ROWS, HID),
        cwg.T,
        ga,
        jnp.swapaxes(gb, 1, 2),
    )


def solution(mesh):
    return jax.shard_map(
        on_device,
        mesh=mesh,
        in_specs=(
            P(("dp", "expert"), None),
            P("dp", "expert", None, None),
            P("expert", None, None),
            P(),
            P(),
            P(("dp", "expert"), None),
            P(("dp", "expert"), None),
            P(("dp", "expert")),
        ),
        out_specs=(
            P("dp", "expert", None, None),
            P("expert", "dp", None),
            P(("dp", "expert"), None),
            P(None, "expert", "dp"),
            P(None, "dp", "expert"),
        ),
        check_vma=False,
    )
```

```python
import functools

import jax
import jax.numpy as jnp
from jax import lax
from jax.experimental import pallas as pl
from jax.experimental.pallas import tpu as pltpu
from jax.sharding import PartitionSpec as P

MESH = pl.DeviceIdType.MESH
F32 = jnp.float32
BF16 = jnp.bfloat16

NX = 4
NY = 4
NE = 16
CAP = 16
TOK = 128
SLOTS = NE * CAP
MODEL = 4096
HID = 768
RANK = 128
EXT = 2 * RANK
ROWS = MODEL // (NX * NY)
ACOL = HID // (NX * NY)

ALL = (4, 1, 1)
STEPS = (
    (2, ALL, 0, 128),
    (2, ALL, 128, 128),
    (1, ALL, 0, 128),
    (3, ALL, 0, 128),
    (1, ALL, 128, 128),
    (3, (1, 0, 2), 128, 128),
    (3, (2, 2, 1), 128, 128),
    (3, (1, 0, 0), 128, 128),
    (0, (3, 1, 1), 0, 128),
    (0, (1, 0, 2), 128, 128),
    (0, (2, 2, 1), 128, 128),
    (0, (1, 0, 0), 0, 128),
    (0, (1, 0, 0), 128, 128),
)
NS = len(STEPS)
HALF = ROWS // 2
PARTS = ((2, 0), (2, 128), (1, 0), (3, 0), (1, 128), (3, 128))
NP = len(PARTS)


def rcopy(src, dst, send, recv, dev):
    return pltpu.make_async_remote_copy(
        src_ref=src, dst_ref=dst, send_sem=send, recv_sem=recv, device_id=dev, device_id_type=MESH
    )


def dot(a, b):
    return jnp.dot(a, b, preferred_element_type=F32)


def dot_t(a, b):
    return lax.dot_general(a, b, (((1,), (1,)), ((), ())), preferred_element_type=F32)


def owner_offset(j, q):
    _, a, b = STEPS[j][1]
    return (a * q + b) % NX


def sent_blocks(j):
    count = STEPS[j][1][0]
    return sum(1 for q in range(count) if owner_offset(j, q))


def blk(p):
    return pl.ds(pl.multiple_of(p * CAP, CAP), CAP)


def kernel(cot_h, hid_h, w_h, ain_h, aout_h, probs_h, routes_h, loop_h, *refs):
    hg_ref, dw_ref, cwg_ref, ga_ref, gb_ref = refs[:5]
    (cot, aout, ain, wm, hx, dx, aperm, pbuf, precv, wv, acc, sel) = refs[5:17]
    probs_ref, routes_ref, loop_ref, gsum = refs[17:21]
    refs = refs[4:]
    (mrow, mxr, mxs, q1s, q1r, q2s, q2r, rzs, rzr, xs, xr, gzs, gzr, ps, pr) = refs[17:32]
    dys = refs[32 : 32 + NS]
    dyr = refs[32 + NS : 32 + 2 * NS]
    tsd = refs[32 + 2 * NS : 32 + 3 * NS]
    trv = refs[32 + 3 * NS : 32 + 4 * NS]
    lsem, z_s, z_r, x_s, x_r, y_s, y_r = refs[32 + 4 * NS :]

    dp = lax.axis_index("dp")
    e = lax.axis_index("expert")
    x = dp // NY
    y = lax.rem(dp, NY)

    def zdev(p):
        return (dp, p)

    def xdev(p):
        return (p * NY + y, e)

    def ydev(p):
        return (x * NY + p, e)

    def z_each(make):
        def one(k, c):
            side = 1 - 2 * lax.rem(k, 2)
            make(lax.rem(e + NE // 2 + side * lax.div(k + 1, 2), NE))
            return c

        lax.fori_loop(0, NE - 1, one, 0)

    def x_each(make):
        for k in range(1, NX):
            make(lax.rem(x + k, NX))

    def y_each(make):
        for k in range(1, NY):
            make(lax.rem(y + k, NY))

    barrier = pltpu.get_barrier_semaphore()
    z_each(lambda p: pl.semaphore_signal(barrier, inc=1, device_id=zdev(p), device_id_type=MESH))
    x_each(lambda p: pl.semaphore_signal(barrier, inc=1, device_id=xdev(p), device_id_type=MESH))
    y_each(lambda p: pl.semaphore_signal(barrier, inc=1, device_id=ydev(p), device_id_type=MESH))

    small = [
        pltpu.make_async_copy(routes_h, routes_ref, lsem.at[5]),
        pltpu.make_async_copy(probs_h, probs_ref, lsem.at[6]),
        pltpu.make_async_copy(loop_h, loop_ref, lsem.at[7]),
    ]
    loads = [
        pltpu.make_async_copy(cot_h, cot, lsem.at[0]),
        pltpu.make_async_copy(aout_h, aout, lsem.at[2]),
        pltpu.make_async_copy(hid_h, hx.at[x], lsem.at[1]),
        pltpu.make_async_copy(ain_h, ain, lsem.at[3]),
        pltpu.make_async_copy(w_h, wm, lsem.at[4]),
    ]
    for one in small + loads:
        one.start()
    for one in small:
        one.wait()

    place = lax.broadcasted_iota(jnp.int32, (NE, CAP, RANK), 1)
    lane = lax.broadcasted_iota(jnp.int32, (NE, CAP, RANK), 2)

    routes = routes_ref[...]
    probs = probs_ref[...].astype(F32)
    expert_id = lax.broadcasted_iota(jnp.int32, (NE, TOK), 0)
    named = jnp.zeros((NE, TOK), F32)
    weight = jnp.zeros((NE, TOK), F32)
    for k in range(8):
        hit = (routes[k : k + 1, :] == expert_id).astype(F32)
        named = named + hit
        weight = weight + hit * probs[k : k + 1, :]
    row = lax.broadcasted_iota(jnp.int32, (TOK, TOK), 0)
    col = lax.broadcasted_iota(jnp.int32, (TOK, TOK), 1)
    before = dot(named.astype(BF16), (row < col).astype(F32).astype(BF16))
    before = jnp.where(named > 0.5, before, -1.0)
    pick3 = (jnp.broadcast_to(before[:, None, :], (NE, CAP, TOK)) == place.astype(F32)).astype(F32)
    pickw = (pick3 * weight[:, None, :]).reshape(SLOTS, TOK)
    sel[...] = pick3.reshape(SLOTS, TOK)
    second = (loop_ref[...] == 1).astype(F32)
    w1 = jnp.sum(pickw * second, axis=1, keepdims=True)
    w0 = jnp.sum(pickw * (1.0 - second), axis=1, keepdims=True)

    def to_rows(column):
        return jnp.broadcast_to(column, (SLOTS, RANK)).reshape(NE, CAP, RANK)

    both = jnp.where(lane == place, to_rows(w0), 0.0) + jnp.where(
        lane == place + CAP, to_rows(w1), 0.0
    )
    mrow[...] = jnp.sum(both, axis=1)[:, None, :]

    def column(j, q):
        off, (_, a, b), start, _ = STEPS[j]
        owner = NY * lax.rem(x + a * q + b, NX) + lax.rem(y + off, NY)
        return pl.multiple_of(owner * ROWS + start, 128)

    def fill(j):
        picked = sel[...].astype(BF16)

        def one(q, c):
            dys[j][q] = dot(picked, cot[:, pl.ds(column(j, q), STEPS[j][3])]).astype(BF16)
            return c

        lax.fori_loop(0, STEPS[j][1][0], one, 0)
        dyr[j][:, blk(e), :] = dys[j][:, blk(e), :]

    most = pl.ds(0, (NE - 1) * CAP)

    def dy_copy(j, p):
        return rcopy(dys[j].at[:, blk(p), :], dyr[j].at[:, blk(e), :], z_s.at[j], z_r.at[j], zdev(p))

    def dy_all(j):
        return rcopy(dys[j].at[:, most, :], dyr[j].at[:, most, :], z_s.at[j], z_r.at[j], zdev(e))

    def pj_copy(p):
        return rcopy(pbuf.at[blk(p), :], precv.at[blk(e), :], z_s.at[NS], z_r.at[NS], zdev(p))

    def pj_all():
        return rcopy(pbuf.at[most, :], precv.at[most, :], z_s.at[NS], z_r.at[NS], zdev(e))

    def zc(n, src, dst, p):
        return rcopy(src.at[p], dst.at[e], z_s.at[NS + n], z_r.at[NS + n], zdev(p))

    def zc_all(n, src, dst):
        part = pl.ds(0, NE - 1)
        return rcopy(src.at[part], dst.at[part], z_s.at[NS + n], z_r.at[NS + n], zdev(e))

    def xc(n, src, dst, p):
        return rcopy(src, dst, x_s.at[n], x_r.at[n], xdev(p))

    def yc(n, src, dst, p):
        return rcopy(src, dst, y_s.at[n], y_r.at[n], ydev(p))

    three = pl.ds(0, 3)

    def h_all():
        return xc(0, hx.at[three], hx.at[three], x)

    def m_all():
        return xc(1, mxr.at[three], mxr.at[three], x)

    def q1_all():
        return yc(0, q1s.at[three], q1r.at[three], y)

    def q2_all():
        return xc(2, q2s.at[three], q2r.at[three], x)

    def t_copy(j, q):
        return xc(3 + j, tsd[j].at[q], trv[j].at[q], lax.rem(x + owner_offset(j, q), NX))

    def t_all(j):
        part = pl.ds(0, sent_blocks(j))
        return xc(3 + j, tsd[j].at[part], trv[j].at[part], x)

    def p_copy(n, p):
        off, start = PARTS[n]
        at = (off - 1, pl.ds(start, HALF))
        return yc(1 + n, ps.at[at], pr.at[at], p)

    loads[0].wait()
    fill(0)
    pl.semaphore_wait(barrier, NE - 1 + 2 * 3)
    z_each(lambda p: dy_copy(0, p).start())
    loads[2].wait()
    x_each(lambda p: xc(0, hx.at[x], hx.at[x], p).start())
    mxr[x, e] = mrow[e]
    z_each(lambda p: rcopy(mrow.at[p], mxr.at[x, e], z_s.at[NS + 1], z_r.at[NS + 1], zdev(p)).start())
    loads[1].wait()
    picked = sel[...].astype(BF16)
    p0 = dot(cot[...], aout[0]).astype(BF16)
    p1 = dot(cot[...], aout[1]).astype(BF16)
    pbuf[...] = jnp.where(w1 > 0.0, dot(picked, p1), dot(picked, p0)).astype(BF16)
    precv[blk(e), :] = pbuf[blk(e), :]
    z_each(lambda p: pj_copy(p).start())
    for j in range(1, NS):
        fill(j)
        z_each(lambda p: dy_copy(j, p).start())

    loads[3].wait()
    for p in range(NE):
        pair = jnp.concatenate(
            [ain[0, 8 * p : 8 * p + 8, :].astype(F32), ain[1, 8 * p : 8 * p + 8, :].astype(F32)], axis=0
        )
        aperm[16 * p : 16 * p + 16, :] = pair.astype(BF16)
    hid = hx[x]

    def weights(s):
        got = jnp.broadcast_to(mxr[s], (NE, CAP, RANK))
        low = jnp.sum(jnp.where(lane == place, got, 0.0), axis=2, keepdims=True)
        high = jnp.sum(jnp.where(lane == place + CAP, got, 0.0), axis=2, keepdims=True)
        low = jnp.broadcast_to(low, (NE, CAP, RANK)).reshape(SLOTS, RANK)
        high = jnp.broadcast_to(high, (NE, CAP, RANK)).reshape(SLOTS, RANK)
        return low, high

    lane2 = lax.broadcasted_iota(jnp.int32, (SLOTS, EXT), 1)
    odd = jnp.bitwise_and(jnp.right_shift(lane2, 3), 1) == 1

    def kept(low, high):
        picked_w = jnp.where(
            odd, jnp.concatenate([high, high], axis=1), jnp.concatenate([low, low], axis=1)
        )
        return picked_w > 0.0

    part = pl.ds(0, NE - 1)
    rcopy(mrow.at[part], mxr.at[x, part], z_s.at[NS + 1], z_r.at[NS + 1], zdev(e)).wait_recv()
    x_each(lambda p: xc(1, mxr.at[x], mxr.at[x], p).start())
    low, high = weights(x)
    wfull = low + high
    wv[...] = wfull
    keep = kept(low, high)
    pj_all().wait_recv()
    proj = precv[...]
    r_at = lax.broadcasted_iota(jnp.int32, (RANK, EXT), 0)
    n_at = lax.broadcasted_iota(jnp.int32, (RANK, EXT), 1)
    spread = jnp.bitwise_or(
        jnp.left_shift(jnp.right_shift(n_at, 4), 3), jnp.bitwise_and(n_at, 7)
    )
    expand = (spread == r_at).astype(F32).astype(BF16)
    wproj = (wfull * proj.astype(F32)).astype(BF16)
    wpm = jnp.where(keep, dot(wproj, expand), 0.0).astype(BF16)
    projm = jnp.where(keep, dot(proj, expand), 0.0).astype(BF16)
    acc[...] = dot(projm, aperm[...])
    qt = lax.dot_general(hid, wpm, (((0,), (0,)), ((), ())), preferred_element_type=F32)
    for d in range(NX * NY):
        q1s[d % NY, d // NY] = qt[ACOL * d : ACOL * (d + 1), :].astype(BF16)
    y_each(lambda p: yc(0, q1s.at[p], q1r.at[y], p).start())

    def arrive(j):
        dy_all(j).wait_recv()

        def one(q, c):
            tsd[j][q] = (dyr[j][q].astype(F32) * wv[...]).T.astype(BF16)
            return c

        lax.fori_loop(0, STEPS[j][1][0], one, 0)
        for q in range(sent_blocks(j)):
            t_copy(j, q).start()
        if j == 0:
            loads[4].wait()
        if j < NS - 1:
            add_grad(j)

    def add_grad(j):
        def two(q, c):
            acc[...] += dot(dyr[j][q], wm[pl.ds(column(j, q), STEPS[j][3]), :])
            return c

        lax.fori_loop(0, STEPS[j][1][0], two, 0)

    def product(j, sums=None):
        if sent_blocks(j):
            t_all(j).wait_recv()
        for q in range(STEPS[j][1][0]):
            back = owner_offset(j, q)
            block = trv[j][q] if back else tsd[j][q]
            s = lax.rem(x + NX - back, NX)
            main, extra = dot(block, hx[s]), dot(block, dx[s])
            sums = (main, extra) if sums is None else (sums[0] + main, sums[1] + extra)
        return sums

    def product_of(off, start, own_first=False):
        steps = [j for j in range(NS) if STEPS[j][0] == off and STEPS[j][2] == start]
        if own_first:
            steps = steps[-1:] + steps[:-1]
        sums = None
        for j in steps:
            sums = product(j, sums)
        return sums

    def reduce_y(n):
        off, start = PARTS[n]
        main, extra = product_of(off, start)
        ps[off - 1, start : start + HALF, :HID] = main.astype(BF16)
        ps[off - 1, start : start + HALF, HID:] = extra.astype(BF16)
        p_copy(n, lax.rem(y + off, NY)).start()

    def gather_y(h):
        start = h * HALF
        for n in range(NP):
            if PARTS[n][1] == start:
                p_copy(n, y).wait_recv()
        rows = slice(start, start + HALF)
        part = pr[0, rows, :].astype(F32) + pr[1, rows, :].astype(F32) + pr[2, rows, :].astype(F32)
        dw_ref[rows, :] = part[:, :HID]
        gsum[...] = part[:, HID:]

    def finish_half(h):
        main, extra = product_of(0, h * HALF, True)
        rows = slice(h * HALF, (h + 1) * HALF)
        gzs[h] = (extra + gsum[...]).T.astype(BF16).reshape(NE, 16, HALF)
        z_each(lambda p: zc(4 + h, gzs.at[h], gzr.at[h], p).start())
        dw_ref[rows, :] += main

    arrive(0)
    arrive(1)
    q1_all().wait_recv()
    total = q1s[y].astype(F32)
    for k in range(1, NY):
        total = total + q1r[lax.rem(y + k, NY)].astype(F32)
    q2s[...] = total.astype(BF16)
    x_each(lambda p: xc(2, q2s.at[p], q2r.at[x], p).start())
    h_all().wait_recv()
    m_all().wait_recv()
    for k in range(NX):
        s = lax.rem(x + k, NX)
        low, high = weights(s)
        dx[s] = jnp.where(kept(low, high), dot_t(hx[s], aperm[...]), 0.0).astype(BF16)
    reduce_y(0)
    arrive(2)
    reduce_y(1)
    arrive(3)
    q2_all().wait_recv()
    total = q2s[x].astype(F32)
    for k in range(1, NX):
        total = total + q2r[lax.rem(x + k, NX)].astype(F32)
    padded = jnp.concatenate([total, jnp.zeros((RANK - ACOL, EXT), F32)], axis=0)
    halves = padded.T.reshape(NE, 2, 8, RANK)
    rzs[...] = (halves[:, 0] + pltpu.roll(halves[:, 1], ACOL, 2)).astype(BF16)
    z_each(lambda p: zc(2, rzs, rzr, p).start())
    reduce_y(2)
    arrive(4)
    reduce_y(3)
    arrive(5)
    arrive(6)
    reduce_y(4)
    arrive(7)
    reduce_y(5)
    arrive(8)
    arrive(9)
    arrive(10)
    gather_y(0)
    arrive(11)
    finish_half(0)
    gather_y(1)
    arrive(12)
    add_grad(12)
    mixed = jnp.sum(hx[x].astype(F32) * acc[...], axis=1, keepdims=True)
    xs[...] = jnp.sum(jnp.where(lane == place, to_rows(mixed), 0.0), axis=1)[:, None, :]
    z_each(lambda p: zc(3, xs, xr, p).start())
    finish_half(1)
    hg_ref[...] = (jnp.concatenate([wv[...]] * (HID // RANK), axis=1) * acc[...]).astype(BF16)

    zc_all(2, rzs, rzr).wait_recv()
    rzr[e] = rzs[e]
    total = jnp.sum(rzr[...].astype(F32), axis=0)
    ga_ref[0] = total[:, :ACOL]
    ga_ref[1] = total[:, ACOL : 2 * ACOL]

    zc_all(3, xs, xr).wait_recv()
    xr[e] = xs[e]
    got = jnp.broadcast_to(xr[...], (NE, CAP, RANK))
    column = jnp.sum(jnp.where(lane == place, got, 0.0), axis=2, keepdims=True)
    per_expert = jnp.sum(sel[...].reshape(NE, CAP, TOK) * column, axis=1)
    for k in range(8):
        hit = routes_ref[k : k + 1, :] == expert_id
        cwg_ref[k : k + 1, :] = jnp.sum(jnp.where(hit, per_expert, 0.0), axis=0, keepdims=True)

    rcopy(mrow.at[part], mxr.at[x, part], z_s.at[NS + 1], z_r.at[NS + 1], zdev(e)).wait_send()
    pj_all().wait_send()
    for j in range(NS):
        dy_all(j).wait_send()
        if sent_blocks(j):
            t_all(j).wait_send()
    h_all().wait_send()
    m_all().wait_send()
    q1_all().wait_send()
    q2_all().wait_send()
    zc_all(2, rzs, rzr).wait_send()
    zc_all(3, xs, xr).wait_send()
    for j in range(NP):
        p_copy(j, y).wait_send()

    for h in range(2):
        zc_all(4 + h, gzs.at[h], gzr.at[h]).wait_recv()
        gzr[h, e] = gzs[h, e]
        total = jnp.sum(gzr[h].astype(F32), axis=0)
        half = slice(h * ROWS // 2, (h + 1) * ROWS // 2)
        gb_ref[0, :, half] = total[:8, :]
        gb_ref[1, :, half] = total[8:, :]
    for h in range(2):
        zc_all(4 + h, gzs.at[h], gzr.at[h]).wait_send()


def store_kernel(*refs):
    ins, outs, sem = refs[:5], refs[5:10], refs[10]
    moves = [pltpu.make_async_copy(a, b, sem.at[n]) for n, (a, b) in enumerate(zip(ins, outs))]
    for one in moves:
        one.start()
    for one in moves:
        one.wait()


def on_device(cotangent, hidden, down_matrix, adapter_in, adapter_out, probs, routes, token_loop):
    vmem = pl.BlockSpec(memory_space=pltpu.VMEM)
    anyw = pl.BlockSpec(memory_space=pl.ANY)
    hbm = pl.BlockSpec(memory_space=pltpu.HBM)
    dims = [(blocks[0], width) for _, blocks, _, width in STEPS]
    scratch = [
        pltpu.VMEM((TOK, MODEL), BF16),
        pltpu.VMEM((2, MODEL, RANK), BF16),
        pltpu.VMEM((2, RANK, HID), BF16),
        pltpu.VMEM((MODEL, HID), BF16),
        pltpu.VMEM((NX, SLOTS, HID), BF16),
        pltpu.VMEM((NX, SLOTS, EXT), BF16),
        pltpu.VMEM((EXT, HID), BF16),
        pltpu.VMEM((SLOTS, RANK), BF16),
        pltpu.VMEM((SLOTS, RANK), BF16),
        pltpu.VMEM((SLOTS, RANK), F32),
        pltpu.VMEM((SLOTS, HID), F32),
        pltpu.VMEM((SLOTS, TOK), F32),
        pltpu.VMEM((8, TOK), BF16),
        pltpu.VMEM((8, TOK), jnp.int32),
        pltpu.VMEM((1, TOK), jnp.int32),
        pltpu.VMEM((HALF, EXT), F32),
        pltpu.VMEM((NE, 1, RANK), F32),
        pltpu.VMEM((NX, NE, 1, RANK), F32),
        pltpu.VMEM((8, RANK), F32),
        pltpu.VMEM((NY, NX, ACOL, EXT), BF16),
        pltpu.VMEM((NY, NX, ACOL, EXT), BF16),
        pltpu.VMEM((NX, ACOL, EXT), BF16),
        pltpu.VMEM((NX, ACOL, EXT), BF16),
        pltpu.VMEM((NE, 8, RANK), BF16),
        pltpu.VMEM((NE, 8, RANK), BF16),
        pltpu.VMEM((NE, 1, RANK), F32),
        pltpu.VMEM((NE, 1, RANK), F32),
        pltpu.VMEM((2, NE, 16, ROWS // 2), BF16),
        pltpu.VMEM((2, NE, 16, ROWS // 2), BF16),
        pltpu.VMEM((3, ROWS, HID + EXT), BF16),
        pltpu.VMEM((3, ROWS, HID + EXT), BF16),
    ]
    scratch += [pltpu.VMEM((n, SLOTS, w), BF16) for n, w in dims]
    scratch += [pltpu.VMEM((n, SLOTS, w), BF16) for n, w in dims]
    scratch += [pltpu.VMEM((n, w, SLOTS), BF16) for n, w in dims]
    scratch += [pltpu.VMEM((n, w, SLOTS), BF16) for n, w in dims]
    sem = pltpu.SemaphoreType.DMA
    scratch += [
        sem((8,)),
        sem((NS + 6,)),
        sem((NS + 6,)),
        sem((3 + NS,)),
        sem((3 + NS,)),
        sem((1 + NP,)),
        sem((1 + NP,)),
    ]
    shapes = (
        ((SLOTS, HID), BF16),
        ((ROWS, HID), F32),
        ((8, TOK), F32),
        ((2, 8, ACOL), F32),
        ((2, 8, ROWS), F32),
    )
    outs = pl.pallas_call(
        kernel,
        out_shape=tuple(pltpu.VMEM(s, t) for s, t in shapes),
        in_specs=[hbm] * 8,
        out_specs=(vmem,) * 5,
        scratch_shapes=scratch,
        compiler_params=pltpu.CompilerParams(
            collective_id=0, has_side_effects=True, vmem_limit_bytes=56 * 2**20
        ),
        name="backward",
    )(
        cotangent,
        hidden.reshape(SLOTS, HID),
        down_matrix.reshape(MODEL, HID),
        adapter_in,
        adapter_out,
        probs.T,
        routes.T,
        token_loop.reshape(1, TOK),
    )
    hg, dw, cwg, ga, gb = pl.pallas_call(
        store_kernel,
        out_shape=tuple(jax.ShapeDtypeStruct(s, t) for s, t in shapes),
        in_specs=[vmem] * 5,
        out_specs=(anyw,) * 5,
        scratch_shapes=[sem((5,))],
        compiler_params=pltpu.CompilerParams(vmem_limit_bytes=4 * 2**20),
        name="store",
    )(*outs)
    return (
        hg.reshape(hidden.shape),
        dw.reshape(1, ROWS, HID),
        cwg.T,
        ga,
        jnp.swapaxes(gb, 1, 2),
    )


def solution(mesh):
    return jax.shard_map(
        on_device,
        mesh=mesh,
        in_specs=(
            P(("dp", "expert"), None),
            P("dp", "expert", None, None),
            P("expert", None, None),
            P(),
            P(),
            P(("dp", "expert"), None),
            P(("dp", "expert"), None),
            P(("dp", "expert")),
        ),
        out_specs=(
            P("dp", "expert", None, None),
            P("expert", "dp", None),
            P(("dp", "expert"), None),
            P(None, "expert", "dp"),
            P(None, "dp", "expert"),
        ),
        check_vma=False,
    )
```

```python
import functools

import jax
import jax.numpy as jnp
from jax import lax
from jax.experimental import pallas as pl
from jax.experimental.pallas import tpu as pltpu
from jax.sharding import PartitionSpec as P

MESH = pl.DeviceIdType.MESH
F32 = jnp.float32
BF16 = jnp.bfloat16

NX = 4
NY = 4
NE = 16
CAP = 16
TOK = 128
SLOTS = NE * CAP
MODEL = 4096
HID = 768
RANK = 128
EXT = 2 * RANK
ROWS = MODEL // (NX * NY)
ACOL = HID // (NX * NY)

ALL = (4, 1, 1)
STEPS = (
    (2, ALL, 0, 128),
    (2, ALL, 128, 128),
    (1, ALL, 0, 128),
    (3, ALL, 0, 128),
    (1, ALL, 128, 128),
    (3, (1, 0, 2), 128, 128),
    (3, (2, 2, 1), 128, 128),
    (3, (1, 0, 0), 128, 128),
    (0, (1, 0, 2), 0, 128),
    (0, (1, 0, 2), 128, 128),
    (0, (2, 2, 1), 0, 128),
    (0, (2, 2, 1), 128, 128),
    (0, (1, 0, 0), 0, 128),
    (0, (1, 0, 0), 128, 128),
)
NS = len(STEPS)
HALF = ROWS // 2
PARTS = ((2, 0), (2, 128), (1, 0), (3, 0), (1, 128), (3, 128))
NP = len(PARTS)


def rcopy(src, dst, send, recv, dev):
    return pltpu.make_async_remote_copy(
        src_ref=src, dst_ref=dst, send_sem=send, recv_sem=recv, device_id=dev, device_id_type=MESH
    )


def dot(a, b):
    return jnp.dot(a, b, preferred_element_type=F32)


def dot_t(a, b):
    return lax.dot_general(a, b, (((1,), (1,)), ((), ())), preferred_element_type=F32)


def owner_offset(j, q):
    _, a, b = STEPS[j][1]
    return (a * q + b) % NX


def sent_blocks(j):
    count = STEPS[j][1][0]
    return sum(1 for q in range(count) if owner_offset(j, q))


def blk(p):
    return pl.ds(pl.multiple_of(p * CAP, CAP), CAP)


def kernel(cot_h, hid_h, w_h, ain_h, aout_h, probs_h, routes_h, loop_h, *refs):
    hg_ref, dw_ref, cwg_ref, ga_ref, gb_ref = refs[:5]
    (cot, aout, ain, wm, hx, dx, aperm, pbuf, precv, wv, acc, sel) = refs[5:17]
    probs_ref, routes_ref, loop_ref, gsum = refs[17:21]
    refs = refs[4:]
    (mrow, mxr, mxs, q1s, q1r, q2s, q2r, rzs, rzr, xs, xr, gzs, gzr, ps, pr) = refs[17:32]
    dys = refs[32 : 32 + NS]
    dyr = refs[32 + NS : 32 + 2 * NS]
    tsd = refs[32 + 2 * NS : 32 + 3 * NS]
    trv = refs[32 + 3 * NS : 32 + 4 * NS]
    lsem, z_s, z_r, x_s, x_r, y_s, y_r = refs[32 + 4 * NS :]

    dp = lax.axis_index("dp")
    e = lax.axis_index("expert")
    x = dp // NY
    y = lax.rem(dp, NY)

    def zdev(p):
        return (dp, p)

    def xdev(p):
        return (p * NY + y, e)

    def ydev(p):
        return (x * NY + p, e)

    def z_each(make):
        def one(k, c):
            side = 1 - 2 * lax.rem(k, 2)
            make(lax.rem(e + NE // 2 + side * lax.div(k + 1, 2), NE))
            return c

        lax.fori_loop(0, NE - 1, one, 0)

    def x_each(make):
        for k in range(1, NX):
            make(lax.rem(x + k, NX))

    def y_each(make):
        for k in range(1, NY):
            make(lax.rem(y + k, NY))

    barrier = pltpu.get_barrier_semaphore()
    for k in range(NE - 1):
        p = lax.rem(e + NE // 2 + (1 - 2 * (k % 2)) * ((k + 1) // 2), NE)
        pl.semaphore_signal(barrier, inc=1, device_id=zdev(p), device_id_type=MESH)
    x_each(lambda p: pl.semaphore_signal(barrier, inc=1, device_id=xdev(p), device_id_type=MESH))
    y_each(lambda p: pl.semaphore_signal(barrier, inc=1, device_id=ydev(p), device_id_type=MESH))

    small = [
        pltpu.make_async_copy(routes_h, routes_ref, lsem.at[5]),
        pltpu.make_async_copy(probs_h, probs_ref, lsem.at[6]),
        pltpu.make_async_copy(loop_h, loop_ref, lsem.at[7]),
    ]
    loads = [
        pltpu.make_async_copy(cot_h, cot, lsem.at[0]),
        pltpu.make_async_copy(aout_h, aout, lsem.at[2]),
        pltpu.make_async_copy(hid_h, hx.at[x], lsem.at[1]),
        pltpu.make_async_copy(ain_h, ain, lsem.at[3]),
        pltpu.make_async_copy(w_h, wm, lsem.at[4]),
    ]
    for one in small + loads:
        one.start()
    for one in small:
        one.wait()

    place = lax.broadcasted_iota(jnp.int32, (NE, CAP, RANK), 1)
    lane = lax.broadcasted_iota(jnp.int32, (NE, CAP, RANK), 2)

    routes = routes_ref[...]
    probs = probs_ref[...].astype(F32)
    expert_id = lax.broadcasted_iota(jnp.int32, (NE, TOK), 0)
    named = jnp.zeros((NE, TOK), F32)
    weight = jnp.zeros((NE, TOK), F32)
    for k in range(8):
        hit = (routes[k : k + 1, :] == expert_id).astype(F32)
        named = named + hit
        weight = weight + hit * probs[k : k + 1, :]
    row = lax.broadcasted_iota(jnp.int32, (TOK, TOK), 0)
    col = lax.broadcasted_iota(jnp.int32, (TOK, TOK), 1)
    before = dot(named.astype(BF16), (row < col).astype(F32).astype(BF16))
    before = jnp.where(named > 0.5, before, -1.0)
    pick3 = (jnp.broadcast_to(before[:, None, :], (NE, CAP, TOK)) == place.astype(F32)).astype(F32)
    sel[...] = pick3.reshape(SLOTS, TOK)

    def to_rows(column):
        return jnp.broadcast_to(column, (SLOTS, RANK)).reshape(NE, CAP, RANK)

    def column(j, q):
        off, (_, a, b), start, _ = STEPS[j]
        owner = NY * lax.rem(x + a * q + b, NX) + lax.rem(y + off, NY)
        return pl.multiple_of(owner * ROWS + start, 128)

    def fill(j):
        picked = sel[...].astype(BF16)

        def one(q, c):
            dys[j][q] = dot(picked, cot[:, pl.ds(column(j, q), STEPS[j][3])]).astype(BF16)
            return c

        lax.fori_loop(0, STEPS[j][1][0], one, 0)
        dyr[j][:, blk(e), :] = dys[j][:, blk(e), :]

    most = pl.ds(0, (NE - 1) * CAP)

    def dy_copy(j, p):
        return rcopy(dys[j].at[:, blk(p), :], dyr[j].at[:, blk(e), :], z_s.at[j], z_r.at[j], zdev(p))

    def dy_all(j):
        return rcopy(dys[j].at[:, most, :], dyr[j].at[:, most, :], z_s.at[j], z_r.at[j], zdev(e))

    def pj_copy(p):
        return rcopy(pbuf.at[blk(p), :], precv.at[blk(e), :], z_s.at[NS], z_r.at[NS], zdev(p))

    def pj_all():
        return rcopy(pbuf.at[most, :], precv.at[most, :], z_s.at[NS], z_r.at[NS], zdev(e))

    def zc(n, src, dst, p):
        return rcopy(src.at[p], dst.at[e], z_s.at[NS + n], z_r.at[NS + n], zdev(p))

    def zc_all(n, src, dst):
        part = pl.ds(0, NE - 1)
        return rcopy(src.at[part], dst.at[part], z_s.at[NS + n], z_r.at[NS + n], zdev(e))

    def xc(n, src, dst, p):
        return rcopy(src, dst, x_s.at[n], x_r.at[n], xdev(p))

    def yc(n, src, dst, p):
        return rcopy(src, dst, y_s.at[n], y_r.at[n], ydev(p))

    three = pl.ds(0, 3)

    def h_all():
        return xc(0, hx.at[three], hx.at[three], x)

    def m_all():
        return xc(1, mxr.at[three], mxr.at[three], x)

    def q1_all():
        return yc(0, q1s.at[three], q1r.at[three], y)

    def q2_all():
        return xc(2, q2s.at[three], q2r.at[three], x)

    def t_copy(j, q):
        return xc(3 + j, tsd[j].at[q], trv[j].at[q], lax.rem(x + owner_offset(j, q), NX))

    def t_all(j):
        part = pl.ds(0, sent_blocks(j))
        return xc(3 + j, tsd[j].at[part], trv[j].at[part], x)

    def p_copy(n, p):
        off, start = PARTS[n]
        at = (off - 1, pl.ds(start, HALF))
        return yc(1 + n, ps.at[at], pr.at[at], p)

    loads[0].wait()
    fill(0)
    pl.semaphore_wait(barrier, NE - 1 + 2 * 3)
    z_each(lambda p: dy_copy(0, p).start())
    loads[2].wait()
    x_each(lambda p: xc(0, hx.at[x], hx.at[x], p).start())
    pickw = (pick3 * weight[:, None, :]).reshape(SLOTS, TOK)
    second = (loop_ref[...] == 1).astype(F32)
    w1 = jnp.sum(pickw * second, axis=1, keepdims=True)
    w0 = jnp.sum(pickw * (1.0 - second), axis=1, keepdims=True)
    both = jnp.where(lane == place, to_rows(w0), 0.0) + jnp.where(
        lane == place + CAP, to_rows(w1), 0.0
    )
    mrow[...] = jnp.sum(both, axis=1)[:, None, :]
    mxr[x, e] = mrow[e]
    z_each(lambda p: rcopy(mrow.at[p], mxr.at[x, e], z_s.at[NS + 1], z_r.at[NS + 1], zdev(p)).start())
    loads[1].wait()
    picked = sel[...].astype(BF16)
    p0 = dot(cot[...], aout[0]).astype(BF16)
    p1 = dot(cot[...], aout[1]).astype(BF16)
    pbuf[...] = jnp.where(w1 > 0.0, dot(picked, p1), dot(picked, p0)).astype(BF16)
    precv[blk(e), :] = pbuf[blk(e), :]
    z_each(lambda p: pj_copy(p).start())
    for j in range(1, NS):
        fill(j)
        z_each(lambda p: dy_copy(j, p).start())

    loads[3].wait()
    for p in range(NE):
        pair = jnp.concatenate(
            [ain[0, 8 * p : 8 * p + 8, :].astype(F32), ain[1, 8 * p : 8 * p + 8, :].astype(F32)], axis=0
        )
        aperm[16 * p : 16 * p + 16, :] = pair.astype(BF16)
    hid = hx[x]

    def weights(s):
        got = jnp.broadcast_to(mxr[s], (NE, CAP, RANK))
        low = jnp.sum(jnp.where(lane == place, got, 0.0), axis=2, keepdims=True)
        high = jnp.sum(jnp.where(lane == place + CAP, got, 0.0), axis=2, keepdims=True)
        low = jnp.broadcast_to(low, (NE, CAP, RANK)).reshape(SLOTS, RANK)
        high = jnp.broadcast_to(high, (NE, CAP, RANK)).reshape(SLOTS, RANK)
        return low, high

    lane2 = lax.broadcasted_iota(jnp.int32, (SLOTS, EXT), 1)
    odd = jnp.bitwise_and(jnp.right_shift(lane2, 3), 1) == 1

    def kept(low, high):
        picked_w = jnp.where(
            odd, jnp.concatenate([high, high], axis=1), jnp.concatenate([low, low], axis=1)
        )
        return picked_w > 0.0

    part = pl.ds(0, NE - 1)
    rcopy(mrow.at[part], mxr.at[x, part], z_s.at[NS + 1], z_r.at[NS + 1], zdev(e)).wait_recv()
    x_each(lambda p: xc(1, mxr.at[x], mxr.at[x], p).start())
    low, high = weights(x)
    wfull = low + high
    wv[...] = wfull
    keep = kept(low, high)
    pj_all().wait_recv()
    proj = precv[...]
    r_at = lax.broadcasted_iota(jnp.int32, (RANK, EXT), 0)
    n_at = lax.broadcasted_iota(jnp.int32, (RANK, EXT), 1)
    spread = jnp.bitwise_or(
        jnp.left_shift(jnp.right_shift(n_at, 4), 3), jnp.bitwise_and(n_at, 7)
    )
    expand = (spread == r_at).astype(F32).astype(BF16)
    wproj = (wfull * proj.astype(F32)).astype(BF16)
    wpm = jnp.where(keep, dot(wproj, expand), 0.0).astype(BF16)
    projm = jnp.where(keep, dot(proj, expand), 0.0).astype(BF16)
    acc[...] = dot(projm, aperm[...])
    qt = lax.dot_general(hid, wpm, (((0,), (0,)), ((), ())), preferred_element_type=F32)
    for d in range(NX * NY):
        q1s[d % NY, d // NY] = qt[ACOL * d : ACOL * (d + 1), :].astype(BF16)
    y_each(lambda p: yc(0, q1s.at[p], q1r.at[y], p).start())

    def arrive(j):
        dy_all(j).wait_recv()

        def one(q, c):
            tsd[j][q] = (dyr[j][q].astype(F32) * wv[...]).T.astype(BF16)
            return c

        lax.fori_loop(0, STEPS[j][1][0], one, 0)
        for q in range(sent_blocks(j)):
            t_copy(j, q).start()
        if j == 0:
            loads[4].wait()
        if j < NS - 1:
            add_grad(j)

    def add_grad(j):
        def two(q, c):
            acc[...] += dot(dyr[j][q], wm[pl.ds(column(j, q), STEPS[j][3]), :])
            return c

        lax.fori_loop(0, STEPS[j][1][0], two, 0)

    def blocks_of(off, start):
        found = []
        for j in range(NS):
            if STEPS[j][0] == off and STEPS[j][2] == start:
                found += [(j, q, owner_offset(j, q)) for q in range(STEPS[j][1][0])]
        return sorted(found, key=lambda entry: (entry[2] > 0, entry[0], entry[1]))

    def product(off, start, right, wait):
        total, seen = None, set()
        for j, q, back in blocks_of(off, start):
            if wait and back and j not in seen:
                t_all(j).wait_recv()
                seen.add(j)
            block = trv[j][q] if back else tsd[j][q]
            term = dot(block, right[lax.rem(x + NX - back, NX)])
            total = term if total is None else total + term
        return total

    def reduce_y(n):
        off, start = PARTS[n]
        main = product(off, start, hx, True)
        extra = product(off, start, dx, False)
        ps[off - 1, start : start + HALF, :HID] = main.astype(BF16)
        ps[off - 1, start : start + HALF, HID:] = extra.astype(BF16)
        p_copy(n, lax.rem(y + off, NY)).start()

    def gather_y(h):
        start = h * HALF
        for n in range(NP):
            if PARTS[n][1] == start:
                p_copy(n, y).wait_recv()
        rows = slice(start, start + HALF)
        part = pr[0, rows, :].astype(F32) + pr[1, rows, :].astype(F32) + pr[2, rows, :].astype(F32)
        dw_ref[rows, :] = part[:, :HID]
        gsum[...] = part[:, HID:]

    def finish_half(h):
        extra = product(0, h * HALF, dx, True)
        gzs[h] = (extra + gsum[...]).T.astype(BF16).reshape(NE, 16, HALF)
        z_each(lambda p: zc(4 + h, gzs.at[h], gzr.at[h], p).start())

    def finish_main(h):
        rows = slice(h * HALF, (h + 1) * HALF)
        dw_ref[rows, :] += product(0, h * HALF, hx, False)

    arrive(0)
    arrive(1)
    q1_all().wait_recv()
    total = q1s[y].astype(F32)
    for k in range(1, NY):
        total = total + q1r[lax.rem(y + k, NY)].astype(F32)
    q2s[...] = total.astype(BF16)
    x_each(lambda p: xc(2, q2s.at[p], q2r.at[x], p).start())
    h_all().wait_recv()
    m_all().wait_recv()
    for k in range(NX):
        s = lax.rem(x + k, NX)
        low, high = weights(s)
        dx[s] = jnp.where(kept(low, high), dot_t(hx[s], aperm[...]), 0.0).astype(BF16)
    reduce_y(0)
    arrive(2)
    reduce_y(1)
    arrive(3)
    q2_all().wait_recv()
    total = q2s[x].astype(F32)
    for k in range(1, NX):
        total = total + q2r[lax.rem(x + k, NX)].astype(F32)
    padded = jnp.concatenate([total, jnp.zeros((RANK - ACOL, EXT), F32)], axis=0)
    halves = padded.T.reshape(NE, 2, 8, RANK)
    rzs[...] = (halves[:, 0] + pltpu.roll(halves[:, 1], ACOL, 2)).astype(BF16)
    z_each(lambda p: zc(2, rzs, rzr, p).start())
    reduce_y(2)
    arrive(4)
    reduce_y(3)
    arrive(5)
    arrive(6)
    reduce_y(4)
    arrive(7)
    arrive(8)
    reduce_y(5)
    arrive(9)
    arrive(10)
    arrive(11)
    gather_y(0)
    arrive(12)
    finish_half(0)
    gather_y(1)
    arrive(13)
    add_grad(13)
    mixed = jnp.sum(hx[x].astype(F32) * acc[...], axis=1, keepdims=True)
    xs[...] = jnp.sum(jnp.where(lane == place, to_rows(mixed), 0.0), axis=1)[:, None, :]
    z_each(lambda p: zc(3, xs, xr, p).start())
    finish_half(1)
    finish_main(0)
    finish_main(1)
    hg_ref[...] = (jnp.concatenate([wv[...]] * (HID // RANK), axis=1) * acc[...]).astype(BF16)

    zc_all(2, rzs, rzr).wait_recv()
    rzr[e] = rzs[e]
    total = jnp.sum(rzr[...].astype(F32), axis=0)
    ga_ref[0] = total[:, :ACOL]
    ga_ref[1] = total[:, ACOL : 2 * ACOL]

    zc_all(3, xs, xr).wait_recv()
    xr[e] = xs[e]
    got = jnp.broadcast_to(xr[...], (NE, CAP, RANK))
    column = jnp.sum(jnp.where(lane == place, got, 0.0), axis=2, keepdims=True)
    per_expert = jnp.sum(sel[...].reshape(NE, CAP, TOK) * column, axis=1)
    for k in range(8):
        hit = routes_ref[k : k + 1, :] == expert_id
        cwg_ref[k : k + 1, :] = jnp.sum(jnp.where(hit, per_expert, 0.0), axis=0, keepdims=True)

    rcopy(mrow.at[part], mxr.at[x, part], z_s.at[NS + 1], z_r.at[NS + 1], zdev(e)).wait_send()
    pj_all().wait_send()
    for j in range(NS):
        dy_all(j).wait_send()
        if sent_blocks(j):
            t_all(j).wait_send()
    h_all().wait_send()
    m_all().wait_send()
    q1_all().wait_send()
    q2_all().wait_send()
    zc_all(2, rzs, rzr).wait_send()
    zc_all(3, xs, xr).wait_send()
    for j in range(NP):
        p_copy(j, y).wait_send()

    for h in range(2):
        zc_all(4 + h, gzs.at[h], gzr.at[h]).wait_recv()
        gzr[h, e] = gzs[h, e]
        total = jnp.sum(gzr[h].astype(F32), axis=0)
        half = slice(h * ROWS // 2, (h + 1) * ROWS // 2)
        gb_ref[0, :, half] = total[:8, :]
        gb_ref[1, :, half] = total[8:, :]
    for h in range(2):
        zc_all(4 + h, gzs.at[h], gzr.at[h]).wait_send()


def store_kernel(*refs):
    ins, outs, sem = refs[:5], refs[5:10], refs[10]
    moves = [pltpu.make_async_copy(a, b, sem.at[n]) for n, (a, b) in enumerate(zip(ins, outs))]
    for one in moves:
        one.start()
    for one in moves:
        one.wait()


def on_device(cotangent, hidden, down_matrix, adapter_in, adapter_out, probs, routes, token_loop):
    vmem = pl.BlockSpec(memory_space=pltpu.VMEM)
    anyw = pl.BlockSpec(memory_space=pl.ANY)
    hbm = pl.BlockSpec(memory_space=pltpu.HBM)
    dims = [(blocks[0], width) for _, blocks, _, width in STEPS]
    scratch = [
        pltpu.VMEM((TOK, MODEL), BF16),
        pltpu.VMEM((2, MODEL, RANK), BF16),
        pltpu.VMEM((2, RANK, HID), BF16),
        pltpu.VMEM((MODEL, HID), BF16),
        pltpu.VMEM((NX, SLOTS, HID), BF16),
        pltpu.VMEM((NX, SLOTS, EXT), BF16),
        pltpu.VMEM((EXT, HID), BF16),
        pltpu.VMEM((SLOTS, RANK), BF16),
        pltpu.VMEM((SLOTS, RANK), BF16),
        pltpu.VMEM((SLOTS, RANK), F32),
        pltpu.VMEM((SLOTS, HID), F32),
        pltpu.VMEM((SLOTS, TOK), F32),
        pltpu.VMEM((8, TOK), BF16),
        pltpu.VMEM((8, TOK), jnp.int32),
        pltpu.VMEM((1, TOK), jnp.int32),
        pltpu.VMEM((HALF, EXT), F32),
        pltpu.VMEM((NE, 1, RANK), F32),
        pltpu.VMEM((NX, NE, 1, RANK), F32),
        pltpu.VMEM((8, RANK), F32),
        pltpu.VMEM((NY, NX, ACOL, EXT), BF16),
        pltpu.VMEM((NY, NX, ACOL, EXT), BF16),
        pltpu.VMEM((NX, ACOL, EXT), BF16),
        pltpu.VMEM((NX, ACOL, EXT), BF16),
        pltpu.VMEM((NE, 8, RANK), BF16),
        pltpu.VMEM((NE, 8, RANK), BF16),
        pltpu.VMEM((NE, 1, RANK), F32),
        pltpu.VMEM((NE, 1, RANK), F32),
        pltpu.VMEM((2, NE, 16, ROWS // 2), BF16),
        pltpu.VMEM((2, NE, 16, ROWS // 2), BF16),
        pltpu.VMEM((3, ROWS, HID + EXT), BF16),
        pltpu.VMEM((3, ROWS, HID + EXT), BF16),
    ]
    scratch += [pltpu.VMEM((n, SLOTS, w), BF16) for n, w in dims]
    scratch += [pltpu.VMEM((n, SLOTS, w), BF16) for n, w in dims]
    scratch += [pltpu.VMEM((n, w, SLOTS), BF16) for n, w in dims]
    scratch += [pltpu.VMEM((n, w, SLOTS), BF16) for n, w in dims]
    sem = pltpu.SemaphoreType.DMA
    scratch += [
        sem((8,)),
        sem((NS + 6,)),
        sem((NS + 6,)),
        sem((3 + NS,)),
        sem((3 + NS,)),
        sem((1 + NP,)),
        sem((1 + NP,)),
    ]
    shapes = (
        ((SLOTS, HID), BF16),
        ((ROWS, HID), F32),
        ((8, TOK), F32),
        ((2, 8, ACOL), F32),
        ((2, 8, ROWS), F32),
    )
    outs = pl.pallas_call(
        kernel,
        out_shape=tuple(pltpu.VMEM(s, t) for s, t in shapes),
        in_specs=[hbm] * 8,
        out_specs=(vmem,) * 5,
        scratch_shapes=scratch,
        compiler_params=pltpu.CompilerParams(
            collective_id=0, has_side_effects=True, vmem_limit_bytes=56 * 2**20
        ),
        name="backward",
    )(
        cotangent,
        hidden.reshape(SLOTS, HID),
        down_matrix.reshape(MODEL, HID),
        adapter_in,
        adapter_out,
        probs.T,
        routes.T,
        token_loop.reshape(1, TOK),
    )
    hg, dw, cwg, ga, gb = pl.pallas_call(
        store_kernel,
        out_shape=tuple(jax.ShapeDtypeStruct(s, t) for s, t in shapes),
        in_specs=[vmem] * 5,
        out_specs=(anyw,) * 5,
        scratch_shapes=[sem((5,))],
        compiler_params=pltpu.CompilerParams(vmem_limit_bytes=4 * 2**20),
        name="store",
    )(*outs)
    return (
        hg.reshape(hidden.shape),
        dw.reshape(1, ROWS, HID),
        cwg.T,
        ga,
        jnp.swapaxes(gb, 1, 2),
    )


def solution(mesh):
    return jax.shard_map(
        on_device,
        mesh=mesh,
        in_specs=(
            P(("dp", "expert"), None),
            P("dp", "expert", None, None),
            P("expert", None, None),
            P(),
            P(),
            P(("dp", "expert"), None),
            P(("dp", "expert"), None),
            P(("dp", "expert")),
        ),
        out_specs=(
            P("dp", "expert", None, None),
            P("expert", "dp", None),
            P(("dp", "expert"), None),
            P(None, "expert", "dp"),
            P(None, "dp", "expert"),
        ),
        check_vma=False,
    )
```

```python
import functools

import jax
import jax.numpy as jnp
from jax import lax
from jax.experimental import pallas as pl
from jax.experimental.pallas import tpu as pltpu
from jax.sharding import PartitionSpec as P

MESH = pl.DeviceIdType.MESH
F32 = jnp.float32
BF16 = jnp.bfloat16

NX = 4
NY = 4
NE = 16
CAP = 16
TOK = 128
SLOTS = NE * CAP
MODEL = 4096
HID = 768
RANK = 128
EXT = 2 * RANK
ROWS = MODEL // (NX * NY)
ACOL = HID // (NX * NY)

ALL = (4, 1, 1)
STEPS = (
    (2, ALL, 0, 128),
    (2, ALL, 128, 128),
    (1, ALL, 0, 128),
    (3, ALL, 0, 128),
    (1, ALL, 128, 128),
    (3, (1, 0, 2), 128, 128),
    (3, (2, 2, 1), 128, 128),
    (3, (1, 0, 0), 128, 128),
    (0, (1, 0, 2), 0, 128),
    (0, (1, 0, 2), 128, 128),
    (0, (2, 2, 1), 0, 128),
    (0, (2, 2, 1), 128, 128),
    (0, (1, 0, 0), 0, 128),
    (0, (1, 0, 0), 128, 128),
)
NS = len(STEPS)
HALF = ROWS // 2
PARTS = ((2, 0), (2, 128), (1, 0), (3, 0), (1, 128), (3, 128))
NP = len(PARTS)


def rcopy(src, dst, send, recv, dev):
    return pltpu.make_async_remote_copy(
        src_ref=src, dst_ref=dst, send_sem=send, recv_sem=recv, device_id=dev, device_id_type=MESH
    )


def dot(a, b):
    return jnp.dot(a, b, preferred_element_type=F32)


def dot_t(a, b):
    return lax.dot_general(a, b, (((1,), (1,)), ((), ())), preferred_element_type=F32)


def owner_offset(j, q):
    _, a, b = STEPS[j][1]
    return (a * q + b) % NX


def sent_blocks(j):
    count = STEPS[j][1][0]
    return sum(1 for q in range(count) if owner_offset(j, q))


def blk(p):
    return pl.ds(pl.multiple_of(p * CAP, CAP), CAP)


def kernel(cot_h, hid_h, w_h, ain_h, aout_h, probs_h, routes_h, loop_h, *refs):
    hg_ref, dw_ref, cwg_ref, ga_ref, gb_ref = refs[:5]
    (cot, aout, ain, wm, hx, dx, aperm, pbuf, precv, wv, acc, sel) = refs[5:17]
    probs_ref, routes_ref, loop_ref, gsum = refs[17:21]
    refs = refs[4:]
    (mrow, mxr, mxs, q1s, q1r, q2s, q2r, rzs, rzr, xs, xr, gzs, gzr, ps, pr) = refs[17:32]
    dys = refs[32 : 32 + NS]
    dyr = refs[32 + NS : 32 + 2 * NS]
    tsd = refs[32 + 2 * NS : 32 + 3 * NS]
    trv = refs[32 + 3 * NS : 32 + 4 * NS]
    lsem, z_s, z_r, x_s, x_r, y_s, y_r = refs[32 + 4 * NS :]

    dp = lax.axis_index("dp")
    e = lax.axis_index("expert")
    x = dp // NY
    y = lax.rem(dp, NY)

    def zdev(p):
        return (dp, p)

    def xdev(p):
        return (p * NY + y, e)

    def ydev(p):
        return (x * NY + p, e)

    def z_each(make):
        def one(k, c):
            side = 1 - 2 * lax.rem(k, 2)
            make(lax.rem(e + NE // 2 + side * lax.div(k + 1, 2), NE))
            return c

        lax.fori_loop(0, NE - 1, one, 0)

    def x_each(make):
        for k in range(1, NX):
            make(lax.rem(x + k, NX))

    def y_each(make):
        for k in range(1, NY):
            make(lax.rem(y + k, NY))

    barrier = pltpu.get_barrier_semaphore()
    for k in range(NE - 1):
        p = lax.rem(e + NE // 2 + (1 - 2 * (k % 2)) * ((k + 1) // 2), NE)
        pl.semaphore_signal(barrier, inc=1, device_id=zdev(p), device_id_type=MESH)
    x_each(lambda p: pl.semaphore_signal(barrier, inc=1, device_id=xdev(p), device_id_type=MESH))
    y_each(lambda p: pl.semaphore_signal(barrier, inc=1, device_id=ydev(p), device_id_type=MESH))

    small = [
        pltpu.make_async_copy(routes_h, routes_ref, lsem.at[5]),
        pltpu.make_async_copy(probs_h, probs_ref, lsem.at[6]),
        pltpu.make_async_copy(loop_h, loop_ref, lsem.at[7]),
    ]
    loads = [
        pltpu.make_async_copy(cot_h, cot, lsem.at[0]),
        pltpu.make_async_copy(aout_h, aout, lsem.at[2]),
        pltpu.make_async_copy(hid_h, hx.at[x], lsem.at[1]),
        pltpu.make_async_copy(ain_h, ain, lsem.at[3]),
        pltpu.make_async_copy(w_h, wm, lsem.at[4]),
    ]
    for one in small + loads:
        one.start()
    for one in small:
        one.wait()

    place = lax.broadcasted_iota(jnp.int32, (NE, CAP, RANK), 1)
    lane = lax.broadcasted_iota(jnp.int32, (NE, CAP, RANK), 2)

    routes = routes_ref[...]
    probs = probs_ref[...].astype(F32)
    expert_id = lax.broadcasted_iota(jnp.int32, (NE, TOK), 0)
    named = jnp.zeros((NE, TOK), F32)
    weight = jnp.zeros((NE, TOK), F32)
    for k in range(8):
        hit = (routes[k : k + 1, :] == expert_id).astype(F32)
        named = named + hit
        weight = weight + hit * probs[k : k + 1, :]
    row = lax.broadcasted_iota(jnp.int32, (TOK, TOK), 0)
    col = lax.broadcasted_iota(jnp.int32, (TOK, TOK), 1)
    before = dot(named.astype(BF16), (row < col).astype(F32).astype(BF16))
    before = jnp.where(named > 0.5, before, -1.0)
    pick3 = (jnp.broadcast_to(before[:, None, :], (NE, CAP, TOK)) == place.astype(F32)).astype(F32)
    sel[...] = pick3.reshape(SLOTS, TOK)

    def to_rows(column):
        return jnp.broadcast_to(column, (SLOTS, RANK)).reshape(NE, CAP, RANK)

    def column(j, q):
        off, (_, a, b), start, _ = STEPS[j]
        owner = NY * lax.rem(x + a * q + b, NX) + lax.rem(y + off, NY)
        return pl.multiple_of(owner * ROWS + start, 128)

    def fill(j):
        picked = sel[...].astype(BF16)

        def one(q, c):
            dys[j][q] = dot(picked, cot[:, pl.ds(column(j, q), STEPS[j][3])]).astype(BF16)
            return c

        lax.fori_loop(0, STEPS[j][1][0], one, 0)
        dyr[j][:, blk(e), :] = dys[j][:, blk(e), :]

    most = pl.ds(0, (NE - 1) * CAP)

    def dy_copy(j, p):
        return rcopy(dys[j].at[:, blk(p), :], dyr[j].at[:, blk(e), :], z_s.at[j], z_r.at[j], zdev(p))

    def dy_all(j):
        return rcopy(dys[j].at[:, most, :], dyr[j].at[:, most, :], z_s.at[j], z_r.at[j], zdev(e))

    def pj_copy(p):
        return rcopy(pbuf.at[blk(p), :], precv.at[blk(e), :], z_s.at[NS], z_r.at[NS], zdev(p))

    def pj_all():
        return rcopy(pbuf.at[most, :], precv.at[most, :], z_s.at[NS], z_r.at[NS], zdev(e))

    def zc(n, src, dst, p):
        return rcopy(src.at[p], dst.at[e], z_s.at[NS + n], z_r.at[NS + n], zdev(p))

    def zc_all(n, src, dst):
        part = pl.ds(0, NE - 1)
        return rcopy(src.at[part], dst.at[part], z_s.at[NS + n], z_r.at[NS + n], zdev(e))

    def xc(n, src, dst, p):
        return rcopy(src, dst, x_s.at[n], x_r.at[n], xdev(p))

    def yc(n, src, dst, p):
        return rcopy(src, dst, y_s.at[n], y_r.at[n], ydev(p))

    three = pl.ds(0, 3)

    def h_all():
        return xc(0, hx.at[three], hx.at[three], x)

    def m_all():
        return xc(1, mxr.at[three], mxr.at[three], x)

    def q1_all():
        return yc(0, q1s.at[three], q1r.at[three], y)

    def q2_all():
        return xc(2, q2s.at[three], q2r.at[three], x)

    def t_copy(j, q):
        return xc(3 + j, tsd[j].at[q], trv[j].at[q], lax.rem(x + owner_offset(j, q), NX))

    def t_all(j):
        part = pl.ds(0, sent_blocks(j))
        return xc(3 + j, tsd[j].at[part], trv[j].at[part], x)

    def p_copy(n, p):
        off, start = PARTS[n]
        at = (off - 1, pl.ds(start, HALF))
        return yc(1 + n, ps.at[at], pr.at[at], p)

    loads[0].wait()
    fill(0)
    pl.semaphore_wait(barrier, NE - 1 + 2 * 3)
    z_each(lambda p: dy_copy(0, p).start())
    loads[2].wait()
    x_each(lambda p: xc(0, hx.at[x], hx.at[x], p).start())
    pickw = (pick3 * weight[:, None, :]).reshape(SLOTS, TOK)
    second = (loop_ref[...] == 1).astype(F32)
    w1 = jnp.sum(pickw * second, axis=1, keepdims=True)
    w0 = jnp.sum(pickw * (1.0 - second), axis=1, keepdims=True)
    both = jnp.where(lane == place, to_rows(w0), 0.0) + jnp.where(
        lane == place + CAP, to_rows(w1), 0.0
    )
    mrow[...] = jnp.sum(both, axis=1)[:, None, :]
    mxr[x, e] = mrow[e]
    z_each(lambda p: rcopy(mrow.at[p], mxr.at[x, e], z_s.at[NS + 1], z_r.at[NS + 1], zdev(p)).start())
    loads[1].wait()
    picked = sel[...].astype(BF16)
    p0 = dot(cot[...], aout[0]).astype(BF16)
    p1 = dot(cot[...], aout[1]).astype(BF16)
    pbuf[...] = jnp.where(w1 > 0.0, dot(picked, p1), dot(picked, p0)).astype(BF16)
    precv[blk(e), :] = pbuf[blk(e), :]
    z_each(lambda p: pj_copy(p).start())
    for j in range(1, NS):
        fill(j)
        z_each(lambda p: dy_copy(j, p).start())

    loads[3].wait()
    for p in range(NE):
        pair = jnp.concatenate(
            [ain[0, 8 * p : 8 * p + 8, :].astype(F32), ain[1, 8 * p : 8 * p + 8, :].astype(F32)], axis=0
        )
        aperm[16 * p : 16 * p + 16, :] = pair.astype(BF16)
    hid = hx[x]

    def weights(s):
        got = jnp.broadcast_to(mxr[s], (NE, CAP, RANK))
        low = jnp.sum(jnp.where(lane == place, got, 0.0), axis=2, keepdims=True)
        high = jnp.sum(jnp.where(lane == place + CAP, got, 0.0), axis=2, keepdims=True)
        low = jnp.broadcast_to(low, (NE, CAP, RANK)).reshape(SLOTS, RANK)
        high = jnp.broadcast_to(high, (NE, CAP, RANK)).reshape(SLOTS, RANK)
        return low, high

    lane2 = lax.broadcasted_iota(jnp.int32, (SLOTS, EXT), 1)
    odd = jnp.bitwise_and(jnp.right_shift(lane2, 3), 1) == 1

    def kept(low, high):
        picked_w = jnp.where(
            odd, jnp.concatenate([high, high], axis=1), jnp.concatenate([low, low], axis=1)
        )
        return picked_w > 0.0

    part = pl.ds(0, NE - 1)
    rcopy(mrow.at[part], mxr.at[x, part], z_s.at[NS + 1], z_r.at[NS + 1], zdev(e)).wait_recv()
    x_each(lambda p: xc(1, mxr.at[x], mxr.at[x], p).start())
    low, high = weights(x)
    wfull = low + high
    wv[...] = wfull
    keep = kept(low, high)
    pj_all().wait_recv()
    proj = precv[...]
    r_at = lax.broadcasted_iota(jnp.int32, (RANK, EXT), 0)
    n_at = lax.broadcasted_iota(jnp.int32, (RANK, EXT), 1)
    spread = jnp.bitwise_or(
        jnp.left_shift(jnp.right_shift(n_at, 4), 3), jnp.bitwise_and(n_at, 7)
    )
    expand = (spread == r_at).astype(F32).astype(BF16)
    wproj = (wfull * proj.astype(F32)).astype(BF16)
    wpm = jnp.where(keep, dot(wproj, expand), 0.0).astype(BF16)
    projm = jnp.where(keep, dot(proj, expand), 0.0).astype(BF16)
    acc[...] = dot(projm, aperm[...])
    qt = lax.dot_general(hid, wpm, (((0,), (0,)), ((), ())), preferred_element_type=F32)
    for d in range(NX * NY):
        q1s[d % NY, d // NY] = qt[ACOL * d : ACOL * (d + 1), :].astype(BF16)
    y_each(lambda p: yc(0, q1s.at[p], q1r.at[y], p).start())

    def arrive(j):
        dy_all(j).wait_recv()

        for q in range(STEPS[j][1][0]):
            tsd[j][q] = (dyr[j][q].astype(F32) * wv[...]).T.astype(BF16)
            if q < sent_blocks(j):
                t_copy(j, q).start()
        if j == 0:
            loads[4].wait()
        if j < NS - 1:
            add_grad(j)

    def add_grad(j):
        def two(q, c):
            acc[...] += dot(dyr[j][q], wm[pl.ds(column(j, q), STEPS[j][3]), :])
            return c

        lax.fori_loop(0, STEPS[j][1][0], two, 0)

    def blocks_of(off, start):
        found = []
        for j in range(NS):
            if STEPS[j][0] == off and STEPS[j][2] == start:
                found += [(j, q, owner_offset(j, q)) for q in range(STEPS[j][1][0])]
        return sorted(found, key=lambda entry: (entry[2] > 0, entry[0], entry[1]))

    def product(off, start, right, wait):
        total, seen = None, set()
        for j, q, back in blocks_of(off, start):
            if wait and back and j not in seen:
                t_all(j).wait_recv()
                seen.add(j)
            block = trv[j][q] if back else tsd[j][q]
            term = dot(block, right[lax.rem(x + NX - back, NX)])
            total = term if total is None else total + term
        return total

    def reduce_y(n):
        off, start = PARTS[n]
        main = product(off, start, hx, True)
        extra = product(off, start, dx, False)
        ps[off - 1, start : start + HALF, :HID] = main.astype(BF16)
        ps[off - 1, start : start + HALF, HID:] = extra.astype(BF16)
        p_copy(n, lax.rem(y + off, NY)).start()

    def gather_y(h):
        start = h * HALF
        for n in range(NP):
            if PARTS[n][1] == start:
                p_copy(n, y).wait_recv()
        rows = slice(start, start + HALF)
        part = pr[0, rows, :].astype(F32) + pr[1, rows, :].astype(F32) + pr[2, rows, :].astype(F32)
        dw_ref[rows, :] = part[:, :HID]
        gsum[...] = part[:, HID:]

    def finish_half(h):
        extra = product(0, h * HALF, dx, True)
        gzs[h] = (extra + gsum[...]).T.astype(BF16).reshape(NE, 16, HALF)
        z_each(lambda p: zc(4 + h, gzs.at[h], gzr.at[h], p).start())

    def finish_main(h):
        rows = slice(h * HALF, (h + 1) * HALF)
        dw_ref[rows, :] += product(0, h * HALF, hx, False)

    arrive(0)
    arrive(1)
    q1_all().wait_recv()
    total = q1s[y].astype(F32)
    for k in range(1, NY):
        total = total + q1r[lax.rem(y + k, NY)].astype(F32)
    q2s[...] = total.astype(BF16)
    x_each(lambda p: xc(2, q2s.at[p], q2r.at[x], p).start())
    h_all().wait_recv()
    m_all().wait_recv()
    for k in range(NX):
        s = lax.rem(x + k, NX)
        low, high = weights(s)
        dx[s] = jnp.where(kept(low, high), dot_t(hx[s], aperm[...]), 0.0).astype(BF16)
    reduce_y(0)
    arrive(2)
    reduce_y(1)
    arrive(3)
    q2_all().wait_recv()
    total = q2s[x].astype(F32)
    for k in range(1, NX):
        total = total + q2r[lax.rem(x + k, NX)].astype(F32)
    padded = jnp.concatenate([total, jnp.zeros((RANK - ACOL, EXT), F32)], axis=0)
    halves = padded.T.reshape(NE, 2, 8, RANK)
    rzs[...] = (halves[:, 0] + pltpu.roll(halves[:, 1], ACOL, 2)).astype(BF16)
    z_each(lambda p: zc(2, rzs, rzr, p).start())
    reduce_y(2)
    arrive(4)
    reduce_y(3)
    arrive(5)
    arrive(6)
    reduce_y(4)
    arrive(7)
    arrive(8)
    reduce_y(5)
    arrive(9)
    arrive(10)
    arrive(11)
    gather_y(0)
    arrive(12)
    finish_half(0)
    gather_y(1)
    arrive(13)
    add_grad(13)
    mixed = jnp.sum(hx[x].astype(F32) * acc[...], axis=1, keepdims=True)
    xs[...] = jnp.sum(jnp.where(lane == place, to_rows(mixed), 0.0), axis=1)[:, None, :]
    z_each(lambda p: zc(3, xs, xr, p).start())
    finish_half(1)
    finish_main(0)
    finish_main(1)
    hg_ref[...] = (jnp.concatenate([wv[...]] * (HID // RANK), axis=1) * acc[...]).astype(BF16)

    zc_all(2, rzs, rzr).wait_recv()
    rzr[e] = rzs[e]
    total = jnp.sum(rzr[...].astype(F32), axis=0)
    ga_ref[0] = total[:, :ACOL]
    ga_ref[1] = total[:, ACOL : 2 * ACOL]

    zc_all(3, xs, xr).wait_recv()
    xr[e] = xs[e]
    got = jnp.broadcast_to(xr[...], (NE, CAP, RANK))
    column = jnp.sum(jnp.where(lane == place, got, 0.0), axis=2, keepdims=True)
    per_expert = jnp.sum(sel[...].reshape(NE, CAP, TOK) * column, axis=1)
    for k in range(8):
        hit = routes_ref[k : k + 1, :] == expert_id
        cwg_ref[k : k + 1, :] = jnp.sum(jnp.where(hit, per_expert, 0.0), axis=0, keepdims=True)

    rcopy(mrow.at[part], mxr.at[x, part], z_s.at[NS + 1], z_r.at[NS + 1], zdev(e)).wait_send()
    pj_all().wait_send()
    for j in range(NS):
        dy_all(j).wait_send()
        if sent_blocks(j):
            t_all(j).wait_send()
    h_all().wait_send()
    m_all().wait_send()
    q1_all().wait_send()
    q2_all().wait_send()
    zc_all(2, rzs, rzr).wait_send()
    zc_all(3, xs, xr).wait_send()
    for j in range(NP):
        p_copy(j, y).wait_send()

    for h in range(2):
        zc_all(4 + h, gzs.at[h], gzr.at[h]).wait_recv()
        gzr[h, e] = gzs[h, e]
        total = jnp.sum(gzr[h].astype(F32), axis=0)
        half = slice(h * ROWS // 2, (h + 1) * ROWS // 2)
        gb_ref[0, :, half] = total[:8, :]
        gb_ref[1, :, half] = total[8:, :]
    for h in range(2):
        zc_all(4 + h, gzs.at[h], gzr.at[h]).wait_send()


def store_kernel(*refs):
    ins, outs, sem = refs[:5], refs[5:10], refs[10]
    moves = [pltpu.make_async_copy(a, b, sem.at[n]) for n, (a, b) in enumerate(zip(ins, outs))]
    for one in moves:
        one.start()
    for one in moves:
        one.wait()


def on_device(cotangent, hidden, down_matrix, adapter_in, adapter_out, probs, routes, token_loop):
    vmem = pl.BlockSpec(memory_space=pltpu.VMEM)
    anyw = pl.BlockSpec(memory_space=pl.ANY)
    hbm = pl.BlockSpec(memory_space=pltpu.HBM)
    dims = [(blocks[0], width) for _, blocks, _, width in STEPS]
    scratch = [
        pltpu.VMEM((TOK, MODEL), BF16),
        pltpu.VMEM((2, MODEL, RANK), BF16),
        pltpu.VMEM((2, RANK, HID), BF16),
        pltpu.VMEM((MODEL, HID), BF16),
        pltpu.VMEM((NX, SLOTS, HID), BF16),
        pltpu.VMEM((NX, SLOTS, EXT), BF16),
        pltpu.VMEM((EXT, HID), BF16),
        pltpu.VMEM((SLOTS, RANK), BF16),
        pltpu.VMEM((SLOTS, RANK), BF16),
        pltpu.VMEM((SLOTS, RANK), F32),
        pltpu.VMEM((SLOTS, HID), F32),
        pltpu.VMEM((SLOTS, TOK), F32),
        pltpu.VMEM((8, TOK), BF16),
        pltpu.VMEM((8, TOK), jnp.int32),
        pltpu.VMEM((1, TOK), jnp.int32),
        pltpu.VMEM((HALF, EXT), F32),
        pltpu.VMEM((NE, 1, RANK), F32),
        pltpu.VMEM((NX, NE, 1, RANK), F32),
        pltpu.VMEM((8, RANK), F32),
        pltpu.VMEM((NY, NX, ACOL, EXT), BF16),
        pltpu.VMEM((NY, NX, ACOL, EXT), BF16),
        pltpu.VMEM((NX, ACOL, EXT), BF16),
        pltpu.VMEM((NX, ACOL, EXT), BF16),
        pltpu.VMEM((NE, 8, RANK), BF16),
        pltpu.VMEM((NE, 8, RANK), BF16),
        pltpu.VMEM((NE, 1, RANK), F32),
        pltpu.VMEM((NE, 1, RANK), F32),
        pltpu.VMEM((2, NE, 16, ROWS // 2), BF16),
        pltpu.VMEM((2, NE, 16, ROWS // 2), BF16),
        pltpu.VMEM((3, ROWS, HID + EXT), BF16),
        pltpu.VMEM((3, ROWS, HID + EXT), BF16),
    ]
    scratch += [pltpu.VMEM((n, SLOTS, w), BF16) for n, w in dims]
    scratch += [pltpu.VMEM((n, SLOTS, w), BF16) for n, w in dims]
    scratch += [pltpu.VMEM((n, w, SLOTS), BF16) for n, w in dims]
    scratch += [pltpu.VMEM((n, w, SLOTS), BF16) for n, w in dims]
    sem = pltpu.SemaphoreType.DMA
    scratch += [
        sem((8,)),
        sem((NS + 6,)),
        sem((NS + 6,)),
        sem((3 + NS,)),
        sem((3 + NS,)),
        sem((1 + NP,)),
        sem((1 + NP,)),
    ]
    shapes = (
        ((SLOTS, HID), BF16),
        ((ROWS, HID), F32),
        ((8, TOK), F32),
        ((2, 8, ACOL), F32),
        ((2, 8, ROWS), F32),
    )
    outs = pl.pallas_call(
        kernel,
        out_shape=tuple(pltpu.VMEM(s, t) for s, t in shapes),
        in_specs=[hbm] * 8,
        out_specs=(vmem,) * 5,
        scratch_shapes=scratch,
        compiler_params=pltpu.CompilerParams(
            collective_id=0, has_side_effects=True, vmem_limit_bytes=56 * 2**20
        ),
        name="backward",
    )(
        cotangent,
        hidden.reshape(SLOTS, HID),
        down_matrix.reshape(MODEL, HID),
        adapter_in,
        adapter_out,
        probs.T,
        routes.T,
        token_loop.reshape(1, TOK),
    )
    hg, dw, cwg, ga, gb = pl.pallas_call(
        store_kernel,
        out_shape=tuple(jax.ShapeDtypeStruct(s, t) for s, t in shapes),
        in_specs=[vmem] * 5,
        out_specs=(anyw,) * 5,
        scratch_shapes=[sem((5,))],
        compiler_params=pltpu.CompilerParams(vmem_limit_bytes=4 * 2**20),
        name="store",
    )(*outs)
    return (
        hg.reshape(hidden.shape),
        dw.reshape(1, ROWS, HID),
        cwg.T,
        ga,
        jnp.swapaxes(gb, 1, 2),
    )


def solution(mesh):
    return jax.shard_map(
        on_device,
        mesh=mesh,
        in_specs=(
            P(("dp", "expert"), None),
            P("dp", "expert", None, None),
            P("expert", None, None),
            P(),
            P(),
            P(("dp", "expert"), None),
            P(("dp", "expert"), None),
            P(("dp", "expert")),
        ),
        out_specs=(
            P("dp", "expert", None, None),
            P("expert", "dp", None),
            P(("dp", "expert"), None),
            P(None, "expert", "dp"),
            P(None, "dp", "expert"),
        ),
        check_vma=False,
    )
```
